32 devices in a mesh: groups: 2 (over x), gx: 16 (over z, y, core).
Axes of the slice: x: 2, y: 2, z: 4, core: 2. Of those that a mesh axis runs over, the one named last changes fastest.
Arguments:
- volume: bfloat16 [32, 256, 6, 128], P('groups', 'gx'), parts along dimension 0, may hold values from -6 to 6
- conv_weight: bfloat16 [256, 27, 128], P('gx'), may hold values from -0.078125 to 0.078125
- conv_bias: float32 [128], replicated, may hold values from -3 to 3
- tconv_weight: bfloat16 [27, 64, 128], replicated, may hold values from -0.25 to 0.25
Outputs:
- decoded: bfloat16 [64, 64, 12, 256], P(('groups', 'gx')), parts along dimension 0
The draws below stay inside these ranges and needn't reach their ends.
There are 2 independent parts, one for each index of `groups`. The reference program is written for one: setup_inputs(seed, part) draws one part's arguments, and reference() takes and returns one part's arrays. A program takes and returns all parts, laid end to end along the dimension named above; an argument that names none is the same for every part. Nothing has to cross between parts.
All inputs are finite; a program needn't handle non-finite values.
Results may differ from the reference program's by a relative error of at most 0.005.
Values may be sent and summed in bfloat16 or wider, within the bound.
A program may use at most 64 MiB of HBM per device.

```python
import jax
import jax.numpy as jnp
from jax import lax

CIN = 256
COUT = 128
CUP = 64
WY = 6
WZ = 128
NX = 16


def raised(values, stream_key, source, target, blocks, factor):
    def block_of(axis_at):
        return (jnp.arange(values.shape[axis_at]) // (values.shape[axis_at] // blocks)).reshape((-1,) + (1,) * (values.ndim - 1 - axis_at))

    one_side = jax.random.permutation(stream_key, blocks)[block_of(target)]
    second = (block_of(target) + blocks // 2) % blocks
    return jnp.where((block_of(source) == one_side) | (block_of(source) == second), factor * values, values)


def block_scale(key, shape, shards, smallest, top_value):
    loudness = 1.0
    for axis_at, shards_of in shards:
        draws = jax.random.uniform(jax.random.fold_in(jax.random.fold_in(key, 6), axis_at), (shards_of,), jnp.float32, smallest / len(shards), top_value / len(shards))
        loudness = loudness * jnp.repeat(jnp.exp(draws), shape[axis_at] // shards_of).reshape((-1,) + (1,) * (len(shape) - 1 - axis_at))
    return loudness


def bell_draw(own_key, extent, width, reach, cuts=(), kind=jnp.bfloat16):
    factor_of = block_scale(own_key, extent, cuts, -0.22, 0.18) if cuts else 1.0
    values = jax.random.normal(own_key, extent, jnp.float32) * width * factor_of
    return jnp.minimum(jnp.maximum(values, -reach), reach).astype(kind)


def bell_draw_with(rng, dims, deviation, reach, shards, heavy, kind=jnp.bfloat16):
    entries = deviation * jax.random.normal(rng, dims, jnp.float32)
    if shards:
        entries = entries * block_scale(rng, dims, shards, -0.22, 0.18)
    return jnp.clip(raised(entries, jax.random.fold_in(rng, 3), *heavy), -reach, reach).astype(kind)


def setup_inputs(seed: int = 0, part: int = 0) -> dict:
    arg_keys = jax.random.split(jax.random.key(seed), 5)
    part_splits = jax.random.split(jax.random.fold_in(arg_keys[4], part), 5)
    volume = bell_draw_with(part_splits[0], (NX, CIN, WY, WZ), 1.0, 6.0, ((1, 16),), (1, 0, 16, 2.0))
    conv_weight = bell_draw(arg_keys[1], (CIN, 27, COUT), (CIN * 27) ** -0.5, 0.078125, ((0, 16),))
    conv_bias = bell_draw(arg_keys[2], (COUT,), 0.5, 3.0, (), jnp.float32)
    tconv_weight = bell_draw(arg_keys[3], (27, CUP, COUT), (COUT * 4) ** -0.5, 0.25)
    return {"volume": volume, "conv_weight": conv_weight, "conv_bias": conv_bias, "tconv_weight": tconv_weight}


def next_cell(field, axis):
    size = field.shape[axis]
    rest = lax.slice_in_dim(field, 1, size, axis=axis)
    zero_shape = list(field.shape)
    zero_shape[axis] = 1
    return jnp.concatenate([rest, jnp.zeros(zero_shape, field.dtype)], axis=axis)


def yz_classes(products, tap_x):
    layout_options = (((1, False),), ((2, False), (0, True)))
    parity_classes = []
    for par_y in range(2):
        for par_z in range(2):
            total = jnp.zeros(products.shape[:1] + products.shape[4:], jnp.float32)
            for tap_y, shift_y in layout_options[par_y]:
                for tap_z, shift_z in layout_options[par_z]:
                    term = products[:, tap_x, tap_y, tap_z]
                    if shift_y:
                        term = next_cell(term, 2)
                    if shift_z:
                        term = next_cell(term, 3)
                    total = total + term
            parity_classes.append(total)
    return jnp.stack(parity_classes, axis=0)


def alternate(even, odd):
    both = jnp.stack([even, odd], axis=0)
    rows, chans, wide_y, wide_z = both.shape[2], both.shape[3], both.shape[4], both.shape[5]
    both = both.reshape(2, 2, 2, rows, chans, wide_y, wide_z)
    both = jnp.transpose(both, (3, 0, 4, 5, 1, 6, 2))
    return both.reshape(2 * rows, chans, 2 * wide_y, 2 * wide_z)


def reference(volume, conv_weight, conv_bias, tconv_weight):
    cin, cout = conv_weight.shape[0], conv_weight.shape[2]
    kernel = conv_weight.reshape(cin, 3, 3, 3, cout)
    kernel = jnp.transpose(kernel, (4, 0, 1, 2, 3))
    lhs = jnp.transpose(volume, (1, 0, 2, 3))[None]
    conv = lax.conv_general_dilated(lhs, kernel, (1, 1, 1), [(1, 1), (1, 1), (1, 1)],
                                    dimension_numbers=("NCDHW", "OIDHW", "NCDHW"),
                                    preferred_element_type=jnp.float32)
    conv = jnp.transpose(conv[0], (1, 0, 2, 3))
    hidden = jnp.maximum(conv + conv_bias[None, :, None, None], 0.0).astype(jnp.bfloat16)
    cup = tconv_weight.shape[1]
    rows, wide_y, wide_z = hidden.shape[0], hidden.shape[2], hidden.shape[3]
    flattened_patches = tconv_weight.reshape(27 * cup, cout).astype(jnp.float32)
    products = jnp.einsum("oc,xcyz->xoyz", flattened_patches, hidden.astype(jnp.float32))
    products = products.reshape(rows, 3, 3, 3, cup, wide_y, wide_z)
    first = yz_classes(products, 0)
    middle = yz_classes(products, 1)
    last = yz_classes(products, 2)
    odd = last + next_cell(first, 1)
    return alternate(middle, odd).astype(jnp.bfloat16)
```

```python
import jax
import jax.numpy as jnp
from jax import lax
from jax.experimental import pallas as pl
from jax.experimental.pallas import tpu as pltpu
from jax.sharding import PartitionSpec as P

MESH = pl.DeviceIdType.MESH
VMEM = pl.BlockSpec(memory_space=pltpu.VMEM)
HBM = pl.BlockSpec(memory_space=pltpu.HBM)


def shift_up(block):
    lane = lax.broadcasted_iota(jnp.int32, block.shape, 1)
    return jnp.where(lane == 0, 0.0, pltpu.roll(block, 1, axis=1))


def shift_down(block):
    size = block.shape[1]
    lane = lax.broadcasted_iota(jnp.int32, block.shape, 1)
    return jnp.where(lane == size - 1, 0.0, pltpu.roll(block, size - 1, axis=1))


def conv_hidden(planes, wide_y, wide_z, tap, bias, first=0, span=None):
    span = span or wide_y
    zero = jnp.zeros_like(planes[0](0))
    total = None
    for kx in range(3):
        padded = jnp.concatenate(
            [zero] + [planes[kx](y) for y in range(wide_y)] + [zero], axis=1
        )
        for ky in range(3):
            weight = jnp.concatenate([tap(kx * 9 + ky * 3 + kz) for kz in range(3)], axis=1)
            cells = padded[:, (ky + first) * wide_z : (ky + first + span) * wide_z]
            term = lax.dot_general(
                weight, cells, (((0,), (0,)), ((), ())), preferred_element_type=jnp.float32
            )
            total = term if total is None else total + term
    cout = total.shape[0] // 3
    rows = []
    for y in range(span):
        part = total[:, y * wide_z : (y + 1) * wide_z]
        rows.append(
            part[cout : 2 * cout]
            + shift_up(part[:cout])
            + shift_down(part[2 * cout :])
            + bias
        )
    return jnp.maximum(jnp.concatenate(rows, axis=1), 0.0).astype(jnp.bfloat16)


BEDS = 4
SPANS = ((0, 2), (2, 4), (4, 6))


def exchange_conv(volume, weight, bias, hidden_out, cells, weights, turned, total, hidden, bias_row,
                  entry_sem, vsend, fsend, vrecv, csend, crecv, wsend, rsend, ysend, xsend, wrecv,
                  msend, mrecv, esend, erecv, known):
    me = lax.axis_index("gx")
    count = lax.axis_size("gx")
    group = lax.axis_index("groups")
    bed, row, core = me // 4, (me // 2) % 2, me % 2
    partner = me + 1 - 2 * core
    wide_y, wide_z = volume.shape[1], volume.shape[3]
    cin = volume.shape[2]
    half = 2 * BEDS * cin
    parts = len(SPANS)
    starts = (row == 0) & (core == 0)
    ends = (row == 1) & (core == 1)

    @pl.when(me == 0)
    def _():
        cells[0] = jnp.zeros(cells.shape[1:], cells.dtype)

    @pl.when(me == count - 1)
    def _():
        cells[5] = jnp.zeros(cells.shape[1:], cells.dtype)
        hidden[1] = jnp.zeros(hidden.shape[1:], hidden.dtype)

    def remote(src, dst, send, recv, target):
        return pltpu.make_async_remote_copy(
            src_ref=src, dst_ref=dst, send_sem=send, recv_sem=recv,
            device_id=target, device_id_type=MESH,
        )

    def arrived(at, sem):
        pltpu.make_async_copy(at, at, sem).wait()

    def index(b, r, c):
        return b * 4 + r * 2 + c

    def slot(b, r, c):
        return pl.ds(pl.multiple_of(((c * 2 + r) * BEDS + b) * cin, cin), cin)

    def other(b, k):
        return (b // 2 + k // 2) % 2 * 2 + (b % 2 + k % 2) % 2

    own = slot(bed, row, core)
    own_cells = pltpu.make_async_copy(
        volume.at[pl.ds(4 * bed, 4)], cells.at[pl.ds(1, 4), :, own], entry_sem.at[0]
    )
    own_weight = pltpu.make_async_copy(weight, weights.at[:, own], entry_sem.at[1])
    own_bias = pltpu.make_async_copy(bias, bias_row, entry_sem.at[2])

    def own_first():
        return pltpu.make_async_copy(
            volume.at[pl.ds(4 * bed - 1, 1)], cells.at[pl.ds(0, 1), :, own], entry_sem.at[3]
        )

    def own_last():
        return pltpu.make_async_copy(
            volume.at[pl.ds(4 * bed + 4, 1)], cells.at[pl.ds(5, 1), :, own], entry_sem.at[3]
        )

    own_cells.start()
    own_weight.start()
    own_bias.start()

    @pl.when(starts & (bed > 0))
    def _():
        own_first().start()

    @pl.when(ends & (bed < BEDS - 1))
    def _():
        own_last().start()

    barrier = pltpu.get_barrier_semaphore()
    reached = (bed > 0).astype(jnp.int32) + (bed < BEDS - 1).astype(jnp.int32) + 2

    def greet(sem):
        def call(target):
            pl.semaphore_signal(sem, inc=1, device_id={"gx": target}, device_id_type=MESH)

        pl.when(bed > 0)(lambda: call(me - 4))
        pl.when(bed < BEDS - 1)(lambda: call(me + 4))
        call(index(bed, 1 - row, core))
        call(partner)

    greet(barrier)
    pl.semaphore_signal(barrier, inc=1, device_id={"groups": 1 - group}, device_id_type=MESH)
    pl.semaphore_wait(barrier, reached + 1)

    def widen(k):
        greet(known.at[k])
        pl.semaphore_wait(known.at[k], reached)

    def centre(b):
        return remote(
            volume.at[pl.ds(4 * b + 1, 2)], cells.at[pl.ds(2, 2), :, own], vsend.at[0, b],
            vrecv.at[0, me], {"gx": index(b, row, core)},
        )

    def turn(b):
        at = cells.at[pl.ds(2, 2), :, slot(b, row, core)]
        src = volume.at[pl.ds(4 * bed + 1, 2)] if b is bed else at
        return remote(
            src, at, fsend.at[b], vrecv.at[0, index(b, row, core)],
            {"gx": index(bed, 1 - row, core)},
        )

    def lower(b):
        return remote(
            volume.at[pl.ds(4 * b, 1)], cells.at[pl.ds(1, 1), :, own], vsend.at[1, b],
            vrecv.at[1, me], {"gx": index(b, 0, core)},
        )

    def upper(b):
        return remote(
            volume.at[pl.ds(4 * b + 3, 1)], cells.at[pl.ds(4, 1), :, own], vsend.at[2, b],
            vrecv.at[1, me], {"gx": index(b, 1, core)},
        )

    def before(b):
        return remote(
            volume.at[pl.ds(4 * b - 1, 1)], cells.at[pl.ds(0, 1), :, own], vsend.at[3, b],
            vrecv.at[2, me], {"gx": index(b, 0, 0)},
        )

    def behind(b):
        return remote(
            volume.at[pl.ds(4 * b + 4, 1)], cells.at[pl.ds(5, 1), :, own], vsend.at[4, b],
            vrecv.at[2, me], {"gx": index(b, 1, 1)},
        )

    taps = weights.shape[0]
    cuts = ((0, (taps + 1) // 2), ((taps + 1) // 2, taps // 2))

    def shard(b, r, c, q):
        return weights.at[pl.ds(*cuts[q]), slot(b, r, c)]

    def direct(q, k, b, r):
        return remote(
            weight.at[pl.ds(*cuts[q])], shard(bed, row, core, q), wsend.at[k],
            wrecv.at[q, bed * 2 + row], {"gx": index(b, r, core)},
        )

    def relay(q, k, b, r):
        at = shard(other(bed, 2), row, core, q)
        return remote(
            at, at, rsend.at[k], wrecv.at[q, other(bed, 2) * 2 + row],
            {"gx": index(b, r, core)},
        )

    def forward(q, b):
        at = shard(b, row, core, q)
        return remote(
            at, at, ysend.at[b], wrecv.at[q, b * 2 + row], {"gx": index(bed, 1 - row, core)}
        )

    def across(q, b, r):
        at = shard(b, r, core, q)
        return remote(
            at, at, xsend.at[b * 2 + r], wrecv.at[q, b * 2 + r], {"groups": 1 - group}
        )

    def beside(q, b, r, mine=False):
        at = shard(b, r, core, q)
        src = weight.at[pl.ds(*cuts[q])] if mine else at
        return remote(
            src, at, msend.at[q, b * 2 + r], mrecv.at[q, b * 2 + r], {"gx": partner}
        )

    near = [(other(bed, 1), row), (bed, 1 - row)]
    mirror = (other(bed, 2), row)
    distant = [(other(bed, 3), row)] + [(other(bed, k), 1 - row) for k in (2, 1, 3)]
    along = [other(bed, k) for k in (2, 1, 3)]

    def by_group(body):
        for g in range(2):
            pl.when(group == g)(lambda g=g: body(g))

    def take(q, b, r):
        arrived(shard(b, r, core, q), wrecv.at[q, b * 2 + r])

    def pass_on(places):
        def body(q):
            for b, r in places:
                take(q, b, r)
                if r is row:
                    forward(q, b).start()
                across(q, b, r).start()
                beside(q, b, r).start()

        by_group(body)

    def pull(places):
        def body(q):
            for b, r in places:
                take(1 - q, b, r)
                beside(1 - q, b, r).start()

        by_group(body)

    @by_group
    def _(q):
        for k, (b, r) in enumerate(near):
            direct(q, 1 + k, b, r).start()

    for q in range(2):
        beside(q, bed, row, True).start()
    turn(bed).start()

    def centres(distance):
        for b in range(BEDS):
            pl.when(jnp.abs(bed - b) == distance)(lambda b=b: centre(b).start())

    centres(1)
    widen(0)

    @by_group
    def _(q):
        direct(q, 0, *mirror).start()

    centres(2)
    widen(1)
    centres(3)
    widen(2)
    widen(3)
    order = [other(bed, k) for k in (2, 3, 1)]

    @by_group
    def _(q):
        take(q, *mirror)
        relay(q, 0, *near[0]).start()
        forward(q, mirror[0]).start()
        across(q, *mirror).start()
        beside(q, *mirror).start()


    def send_lower(act):
        for b in order + [bed]:
            pl.when(index(b, 0, core) != me)(lambda b=b: act(lower(b)))
        for b in order + [bed]:
            pl.when((index(b, 0, 0) != me) & (b > 0))(lambda b=b: act(before(b)))

    def send_upper(act):
        for b in order + [bed]:
            pl.when(index(b, 1, core) != me)(lambda b=b: act(upper(b)))
        for b in order + [bed]:
            pl.when((index(b, 1, 1) != me) & (b < BEDS - 1))(lambda b=b: act(behind(b)))

    pass_on(near)
    send_lower(lambda copy: copy.start())
    send_upper(lambda copy: copy.start())
    pass_on(distant[:1])
    for b in order[::-1]:
        arrived(cells.at[pl.ds(2, 2), :, slot(b, row, core)], vrecv.at[0, index(b, row, core)])
        turn(b).start()
    own_cells.wait()

    def quarter(r, c):
        return pl.ds(pl.multiple_of((c * 2 + r) * BEDS * cin, BEDS * cin), BEDS * cin)

    def mate(k):
        if k < 2:
            at = cells.at[pl.ds(2, 2), :, quarter(row if k == 0 else 1 - row, core)]
        else:
            at = cells.at[pl.ds(1 + 3 * row, 1), :, pl.ds(pl.multiple_of(core * half, half), half)]
        return remote(at, at, csend.at[k], crecv.at[k], {"gx": partner})

    def mated(k):
        if k < 2:
            at = cells.at[pl.ds(2, 2), :, quarter(row if k == 0 else 1 - row, 1 - core)]
        else:
            at = cells.at[
                pl.ds(1 + 3 * row, 1), :, pl.ds(pl.multiple_of((1 - core) * half, half), half)
            ]
        arrived(at, crecv.at[k])

    mate(0).start()
    pass_on(distant[1:])
    pull([mirror] + near)
    for b in [bed] + order[::-1]:
        arrived(
            cells.at[pl.ds(2, 2), :, slot(b, 1 - row, core)],
            vrecv.at[0, index(b, 1 - row, core)],
        )
    mate(1).start()
    pull(distant)
    for b in [bed] + order[::-1]:
        for r in range(2):
            @pl.when(index(b, r, core) != me)
            def _(b=b, r=r):
                arrived(
                    cells.at[pl.ds(1 + 3 * row, 1), :, slot(b, r, core)],
                    vrecv.at[1, index(b, r, core)],
                )
    mate(2).start()

    own_weight.wait()
    own_bias.wait()
    cout = weights.shape[2]
    for b in range(BEDS):
        for r in range(2):
            for q in range(2):
                arrived(shard(b, r, 1 - core, q), mrecv.at[q, b * 2 + r])
    for tap in range(taps):
        kx, ky, kz = tap // 9, tap // 3 % 3, tap % 3
        turned[kx, pl.ds(kz * cout, cout), pl.ds(ky * 2 * half, 2 * half)] = jnp.transpose(
            weights[tap]
        )
    for k in range(3):
        mated(k)

    local = 1 + row * 2 + core

    def product(kx, low, high):
        zero = jnp.zeros((2 * half, wide_z), cells.dtype)
        sides = []
        for ky in range(3):
            found = [
                cells[local - 1 + kx, y + ky - 1] if 0 <= y + ky - 1 < wide_y else zero
                for y in range(low, high)
            ]
            sides.append(jnp.concatenate(found, axis=1))
        return jnp.dot(
            turned[kx], jnp.concatenate(sides, axis=0), preferred_element_type=jnp.float32
        )

    for low, high in SPANS:
        total[:, pl.ds(low * wide_z, (high - low) * wide_z)] = product(
            1, low, high
        ) + product(2 - 2 * core, low, high)

    @pl.when(starts & (bed > 0))
    def _():
        own_first().wait()

    @pl.when(ends & (bed < BEDS - 1))
    def _():
        own_last().wait()

    for last, needed in ((0, starts & (bed > 0)), (5, ends & (bed < BEDS - 1))):
        @pl.when(needed)
        def _(last=last):
            for b in [bed] + order[::-1]:
                for r in range(2):
                    for c in range(2):
                        @pl.when(index(b, r, c) != me)
                        def _(b=b, r=r, c=c):
                            arrived(
                                cells.at[pl.ds(last, 1), :, slot(b, r, c)],
                                vrecv.at[2, index(b, r, c)],
                            )

    def edge(k):
        low, high = SPANS[k]
        at = pl.ds(low, high - low)
        return remote(
            hidden.at[0, at], hidden.at[1, at], esend.at[k], erecv.at[k], {"gx": me - 1}
        )

    bias_cells = jnp.transpose(jnp.broadcast_to(bias_row[...], (wide_z, cout)))
    for k, (low, high) in enumerate(SPANS):
        final = total[:, pl.ds(low * wide_z, (high - low) * wide_z)] + product(2 * core, low, high)
        for y in range(low, high):
            part = final[:, (y - low) * wide_z : (y - low + 1) * wide_z]
            hidden[0, y] = jnp.maximum(
                part[cout : 2 * cout]
                + shift_up(part[:cout])
                + shift_down(part[2 * cout :])
                + bias_cells,
                0.0,
            ).astype(jnp.bfloat16)

        @pl.when(me > 0)
        def _(k=k):
            edge(k).start()

    @by_group
    def _(q):
        direct(q, 0, *mirror).wait_send()
        for k, (b, r) in enumerate(near):
            direct(q, 1 + k, b, r).wait_send()
        relay(q, 0, *near[0]).wait_send()
        for b in along:
            forward(q, b).wait_send()
        for b, r in [mirror] + near + distant:
            across(q, b, r).wait_send()

    for q in range(2):
        beside(q, bed, row, True).wait_send()
        for b, r in [mirror] + near + distant:
            beside(q, b, r).wait_send()

    for b in order:
        centre(b).wait_send()
        turn(b).wait_send()
    turn(bed).wait_send()
    send_lower(lambda copy: copy.wait_send())
    send_upper(lambda copy: copy.wait_send())
    for k in range(3):
        mate(k).wait_send()

    @pl.when(me < count - 1)
    def _():
        for k, (low, high) in enumerate(SPANS):
            arrived(hidden.at[1, pl.ds(low, high - low)], erecv.at[k])

    @pl.when(me > 0)
    def _():
        for k in range(parts):
            edge(k).wait_send()

    hidden_out[...] = hidden[...]


def local_conv(planes, weight, bias, hidden_out):
    wide_y, wide_z = planes.shape[1], planes.shape[3]
    cells = [lambda y, kx=kx: planes[kx, y] for kx in range(3)]
    hidden_out[...] = conv_hidden(cells, wide_y, wide_z, lambda t: weight[t], bias[...])


def transposed(hidden, tconv, out):
    wide_z = out.shape[3] // 2
    wide_y = out.shape[1] // 2
    cup = tconv.shape[1]
    cout = tconv.shape[2]
    here, after = (
        jnp.concatenate([hidden[i, y] for y in range(wide_y)], axis=1) for i in range(2)
    )

    def down(x):
        return jnp.concatenate([x[:, wide_z:], jnp.zeros_like(x[:, :wide_z])], axis=1)

    def taps(kx, ky):
        t = kx * 9 + ky * 3
        return tconv[t : t + 3].reshape(3 * cup, cout)

    row = lax.broadcasted_iota(jnp.int32, (2 * wide_z, 2 * wide_z), 0)
    col = lax.broadcasted_iota(jnp.int32, (2 * wide_z, 2 * wide_z), 1)
    spread = jnp.where(
        col == jnp.where(row < wide_z, 2 * row, 2 * (row - wide_z) + 1), 1.0, 0.0
    ).astype(jnp.bfloat16)
    x_options = (((1, here),), ((2, here), (0, after)))
    for pu in range(2):
        for pv in range(2):
            left, right = [], []
            for kx, field in x_options[pu]:
                for ky, shifted in (((1, False),), ((2, False), (0, True)))[pv]:
                    left.append(taps(kx, ky))
                    right.append(down(field) if shifted else field)
            product = jnp.dot(
                jnp.concatenate(left, axis=1), jnp.concatenate(right, axis=0),
                preferred_element_type=jnp.float32,
            )
            pairs = []
            for y in range(wide_y):
                part = product[:, y * wide_z : (y + 1) * wide_z]
                even = part[cup : 2 * cup]
                odd = part[2 * cup :] + shift_down(part[:cup])
                pairs.append(jnp.concatenate([even, odd], axis=1).astype(jnp.bfloat16))
            mixed = jnp.dot(
                jnp.concatenate(pairs, axis=0), spread, preferred_element_type=jnp.float32
            ).astype(jnp.bfloat16)
            for y in range(wide_y):
                out[pu, 2 * y + pv] = mixed[y * cup : (y + 1) * cup]


def native_hidden(volume, conv_weight, bias):
    count = lax.axis_size("gx")
    forward = [(i, i + 1) for i in range(count - 1)]
    backward = [(i + 1, i) for i in range(count - 1)]
    local = lax.all_to_all(volume, "gx", split_axis=0, concat_axis=1, tiled=True)
    weight = lax.all_gather(conv_weight, "gx", axis=0, tiled=True)
    rows = local.shape[0]
    low = lax.ppermute(local[rows - 1 :], "gx", forward)
    high = lax.ppermute(local[:1], "gx", backward)
    planes = jnp.transpose(jnp.concatenate([low, local, high], axis=0), (0, 2, 1, 3))
    weight = jnp.transpose(weight, (1, 0, 2))
    cout = weight.shape[2]
    shape = jax.ShapeDtypeStruct((cout, planes.shape[1] * planes.shape[3]), jnp.bfloat16)
    conv = pl.pallas_call(
        local_conv, out_shape=shape, in_specs=[VMEM] * 3, out_specs=VMEM,
        compiler_params=pltpu.CompilerParams(vmem_limit_bytes=40 << 20),
    )
    hidden = [conv(planes[r : r + 3], weight, bias) for r in range(rows)]
    hidden.append(lax.ppermute(hidden[0], "gx", backward))
    wide_y, wide_z = volume.shape[2], volume.shape[3]
    hidden = [
        jnp.transpose(plane.reshape(cout, wide_y, wide_z), (1, 0, 2)) for plane in hidden
    ]
    return [jnp.stack(hidden[r : r + 2]) for r in range(rows)]


def remote_hidden(volume, conv_weight, bias):
    count = lax.axis_size("gx")
    cells = jnp.transpose(volume, (0, 2, 1, 3))
    weight = jnp.transpose(conv_weight, (1, 0, 2))
    taps, cin, cout = weight.shape
    wide_y, wide_z = cells.shape[1], cells.shape[3]
    wide = count * cin
    chips = count // 2
    parts = len(SPANS)
    dma = pltpu.SemaphoreType.DMA
    hidden = pl.pallas_call(
        exchange_conv,
        out_shape=jax.ShapeDtypeStruct((2, wide_y, cout, wide_z), jnp.bfloat16),
        in_specs=[HBM, HBM, HBM],
        out_specs=VMEM,
        scratch_shapes=[
            pltpu.VMEM((6, wide_y, wide, wide_z), jnp.bfloat16),
            pltpu.VMEM((taps, wide, cout), jnp.bfloat16),
            pltpu.VMEM((3, 3 * cout, 3 * wide), jnp.bfloat16),
            pltpu.VMEM((3 * cout, wide_y * wide_z), jnp.float32),
            pltpu.VMEM((2, wide_y, cout, wide_z), jnp.bfloat16),
            pltpu.VMEM((1, cout), jnp.float32),
            dma((4,)),
            dma((5, BEDS)), dma((BEDS,)), dma((3, count)),
            dma((3,)), dma((3,)),
            dma((3,)), dma((1,)), dma((BEDS,)), dma((chips,)), dma((2, chips)),
            dma((2, chips)), dma((2, chips)),
            dma((parts,)), dma((parts,)),
            pltpu.SemaphoreType.REGULAR((4,)),
        ],
        compiler_params=pltpu.CompilerParams(
            collective_id=0, has_side_effects=True, vmem_limit_bytes=60 << 20
        ),
    )(cells, weight, bias.reshape(1, cout))
    return [hidden]


def per_device(volume, conv_weight, conv_bias, tconv_weight):
    count = lax.axis_size("gx")
    rows = volume.shape[0] // count
    bias = conv_bias[:, None]
    suited = (
        rows == 1 and count == 16 and lax.axis_size("groups") == 2
        and volume.shape[1] % 16 == 0 and volume.shape[2] == SPANS[-1][1]
    )
    hidden = (remote_hidden if suited else native_hidden)(volume, conv_weight, bias)
    cup = tconv_weight.shape[1]
    shape = jax.ShapeDtypeStruct(
        (2, 2 * volume.shape[2], cup, 2 * volume.shape[3]), jnp.bfloat16
    )
    tconv = pl.pallas_call(
        transposed, out_shape=shape, in_specs=[VMEM] * 2, out_specs=VMEM,
        compiler_params=pltpu.CompilerParams(vmem_limit_bytes=40 << 20),
    )
    outs = [tconv(planes, tconv_weight) for planes in hidden]
    out = outs[0] if len(outs) == 1 else jnp.concatenate(outs, axis=0)
    return jnp.transpose(out, (0, 2, 1, 3))


def solution(mesh):
    return jax.shard_map(
        per_device,
        mesh=mesh,
        in_specs=(P("groups", "gx", None, None), P("gx", None, None), P(), P()),
        out_specs=P(("groups", "gx"), None, None, None),
        check_vma=False,
    )
```

```python
import jax
import jax.numpy as jnp
from jax import lax
from jax.experimental import pallas as pl
from jax.experimental.pallas import tpu as pltpu
from jax.sharding import PartitionSpec as P

MESH = pl.DeviceIdType.MESH
VMEM = pl.BlockSpec(memory_space=pltpu.VMEM)
HBM = pl.BlockSpec(memory_space=pltpu.HBM)


def shift_up(block):
    lane = lax.broadcasted_iota(jnp.int32, block.shape, 1)
    return jnp.where(lane == 0, 0.0, pltpu.roll(block, 1, axis=1))


def shift_down(block):
    size = block.shape[1]
    lane = lax.broadcasted_iota(jnp.int32, block.shape, 1)
    return jnp.where(lane == size - 1, 0.0, pltpu.roll(block, size - 1, axis=1))


def conv_hidden(planes, wide_y, wide_z, tap, bias, first=0, span=None):
    span = span or wide_y
    zero = jnp.zeros_like(planes[0](0))
    total = None
    for kx in range(3):
        padded = jnp.concatenate(
            [zero] + [planes[kx](y) for y in range(wide_y)] + [zero], axis=1
        )
        for ky in range(3):
            weight = jnp.concatenate([tap(kx * 9 + ky * 3 + kz) for kz in range(3)], axis=1)
            cells = padded[:, (ky + first) * wide_z : (ky + first + span) * wide_z]
            term = lax.dot_general(
                weight, cells, (((0,), (0,)), ((), ())), preferred_element_type=jnp.float32
            )
            total = term if total is None else total + term
    cout = total.shape[0] // 3
    rows = []
    for y in range(span):
        part = total[:, y * wide_z : (y + 1) * wide_z]
        rows.append(
            part[cout : 2 * cout]
            + shift_up(part[:cout])
            + shift_down(part[2 * cout :])
            + bias
        )
    return jnp.maximum(jnp.concatenate(rows, axis=1), 0.0).astype(jnp.bfloat16)


BEDS = 4
SPANS = ((0, 3), (3, 5), (5, 6))
LAST = ((0, 2), (2, 4), (4, 6))


def exchange_conv(volume, weight, bias, tconv, out, cells, weights, turned, total, hidden, bias_row,
                  fan, decoded, out_sem,
                  entry_sem, csem_send, centre_recv, turn_recv, level_send, level_recv, outer_send,
                  outer_recv, csend, crecv, wsend, wrecv, xrecv, msend, mrecv, esend, erecv, known):
    me = lax.axis_index("gx")
    count = lax.axis_size("gx")
    group = lax.axis_index("groups")
    bed, row, core = me // 4, (me // 2) % 2, me % 2
    partner = me + 1 - 2 * core
    wide_y, wide_z = volume.shape[1], volume.shape[3]
    cin = volume.shape[2]
    half = 2 * BEDS * cin
    parts = len(SPANS)
    starts = (row == 0) & (core == 0)
    ends = (row == 1) & (core == 1)

    @pl.when(me == 0)
    def _():
        cells[0] = jnp.zeros(cells.shape[1:], cells.dtype)

    @pl.when(me == count - 1)
    def _():
        cells[5] = jnp.zeros(cells.shape[1:], cells.dtype)
        hidden[1] = jnp.zeros(hidden.shape[1:], hidden.dtype)

    def remote(src, dst, send, recv, target):
        return pltpu.make_async_remote_copy(
            src_ref=src, dst_ref=dst, send_sem=send, recv_sem=recv,
            device_id=target, device_id_type=MESH,
        )

    def arrived(at, sem):
        pltpu.make_async_copy(at, at, sem).wait()

    def index(b, r, c):
        return b * 4 + r * 2 + c

    def slot(b, r, c):
        return pl.ds(pl.multiple_of(((c * 2 + r) * BEDS + b) * cin, cin), cin)

    def other(b, k):
        return (b // 2 + k // 2) % 2 * 2 + (b % 2 + k % 2) % 2

    own = slot(bed, row, core)
    own_cells = pltpu.make_async_copy(
        volume.at[pl.ds(4 * bed, 4)], cells.at[pl.ds(1, 4), :, own], entry_sem.at[0]
    )
    own_weight = pltpu.make_async_copy(weight, weights.at[:, own], entry_sem.at[1])
    own_bias = pltpu.make_async_copy(bias, bias_row, entry_sem.at[2])

    def own_first():
        return pltpu.make_async_copy(
            volume.at[pl.ds(4 * bed - 1, 1)], cells.at[pl.ds(0, 1), :, own], entry_sem.at[3]
        )

    def own_last():
        return pltpu.make_async_copy(
            volume.at[pl.ds(4 * bed + 4, 1)], cells.at[pl.ds(5, 1), :, own], entry_sem.at[3]
        )

    own_cells.start()
    own_weight.start()
    own_bias.start()
    own_fan = pltpu.make_async_copy(tconv, fan, entry_sem.at[4])
    own_fan.start()

    @pl.when(starts & (bed > 0))
    def _():
        own_first().start()

    @pl.when(ends & (bed < BEDS - 1))
    def _():
        own_last().start()

    barrier = pltpu.get_barrier_semaphore()
    reached = (bed > 0).astype(jnp.int32) + (bed < BEDS - 1).astype(jnp.int32) + 2

    def greet(sem):
        def call(target):
            pl.semaphore_signal(sem, inc=1, device_id={"gx": target}, device_id_type=MESH)

        pl.when(bed > 0)(lambda: call(me - 4))
        pl.when(bed < BEDS - 1)(lambda: call(me + 4))
        call(index(bed, 1 - row, core))
        call(partner)

    greet(barrier)
    pl.semaphore_signal(barrier, inc=1, device_id={"groups": 1 - group}, device_id_type=MESH)
    pl.semaphore_wait(barrier, reached + 1)

    def widen(k):
        greet(known.at[k])
        pl.semaphore_wait(known.at[k], reached)

    def centre(b):
        return remote(
            volume.at[pl.ds(4 * b + 1, 2)], cells.at[pl.ds(2, 2), :, own], csem_send,
            centre_recv.at[bed], {"gx": index(b, row, core)},
        )

    def turn(b):
        at = cells.at[pl.ds(2, 2), :, slot(b, row, core)]
        src = volume.at[pl.ds(4 * bed + 1, 2)] if b is bed else at
        return remote(src, at, csem_send, turn_recv, {"gx": index(bed, 1 - row, core)})

    def level(b, plane, near_plane, r):
        return remote(
            volume.at[pl.ds(4 * b + plane, 1)], cells.at[pl.ds(near_plane, 1), :, own], level_send,
            level_recv, {"gx": index(b, r, core)},
        )

    def outer(b, plane, near_plane, r):
        return remote(
            volume.at[pl.ds(4 * b + plane, 1)], cells.at[pl.ds(near_plane, 1), :, own], outer_send,
            outer_recv, {"gx": index(b, r, r)},
        )

    taps = weights.shape[0]
    cuts = ((0, (taps + 1) // 2), ((taps + 1) // 2, taps // 2))

    def shard(b, r, c, q):
        return weights.at[pl.ds(*cuts[q]), slot(b, r, c)]

    def direct(q, b, r):
        return remote(
            weight.at[pl.ds(*cuts[q])], shard(bed, row, core, q), wsend, wrecv.at[bed * 2 + row],
            {"gx": index(b, r, core)},
        )

    def relay(q, b, r):
        at = shard(other(bed, 2), row, core, q)
        return remote(
            at, at, wsend, wrecv.at[other(bed, 2) * 2 + row], {"gx": index(b, r, core)}
        )

    def across(q, b, r):
        at = shard(b, r, core, q)
        return remote(at, at, wsend, xrecv, {"groups": 1 - group})

    def side(c):
        return pl.ds(pl.multiple_of(c * half, half), half)

    def beside(q):
        at = weights.at[pl.ds(*cuts[q]), side(core)]
        return remote(at, at, msend.at[q], mrecv.at[q], {"gx": partner})

    near = [(other(bed, 1), row), (other(bed, 1), 1 - row), (bed, 1 - row)]
    mirror = (other(bed, 2), row)
    distant = [(other(bed, 3), row), (other(bed, 3), 1 - row), (other(bed, 2), 1 - row)]

    def by_group(body):
        for g in range(2):
            pl.when(group == g)(lambda g=g: body(g))

    def take(q, b, r):
        arrived(shard(b, r, core, q), wrecv.at[b * 2 + r])

    def pass_on(places):
        def body(q):
            for b, r in places:
                take(q, b, r)
                across(q, b, r).start()

        by_group(body)

    @by_group
    def _(q):
        direct(q, *near[0]).start()
        direct(q, *near[2]).start()

    turn(bed).start()

    def centres(distance):
        for b in range(BEDS):
            pl.when(jnp.abs(bed - b) == distance)(lambda b=b: centre(b).start())

    centres(1)
    widen(0)

    @by_group
    def _(q):
        direct(q, *mirror).start()
        direct(q, *near[1]).start()

    centres(2)
    widen(1)
    centres(3)
    widen(2)
    widen(3)
    order = [other(bed, k) for k in (2, 3, 1)]

    @by_group
    def _(q):
        take(q, *mirror)
        for b, r in near:
            relay(q, b, r).start()
        across(q, *mirror).start()

    for b in order + [bed]:
        pl.when(index(b, 0, core) != me)(lambda b=b: level(b, 0, 1, 0).start())
    for b in order + [bed]:
        pl.when((index(b, 0, 0) != me) & (b > 0))(lambda b=b: outer(b, -1, 0, 0).start())
    for b in order + [bed]:
        pl.when(index(b, 1, core) != me)(lambda b=b: level(b, 3, 4, 1).start())
    for b in order + [bed]:
        pl.when((index(b, 1, 1) != me) & (b < BEDS - 1))(lambda b=b: outer(b, 4, 5, 1).start())

    pass_on(near)
    for b in order[::-1]:
        arrived(cells.at[pl.ds(2, 2), :, slot(b, row, core)], centre_recv.at[b])
        turn(b).start()
    own_cells.wait()

    def quarter(r, c):
        return pl.ds(pl.multiple_of((c * 2 + r) * BEDS * cin, BEDS * cin), BEDS * cin)

    def mate(k):
        if k < 2:
            at = cells.at[pl.ds(2, 2), :, quarter(row if k == 0 else 1 - row, core)]
        else:
            at = cells.at[pl.ds(1 + 3 * row, 1), :, side(core)]
        return remote(at, at, csend.at[k], crecv.at[k], {"gx": partner})

    def mated(k):
        if k < 2:
            at = cells.at[pl.ds(2, 2), :, quarter(row if k == 0 else 1 - row, 1 - core)]
        else:
            at = cells.at[pl.ds(1 + 3 * row, 1), :, side(1 - core)]
        arrived(at, crecv.at[k])

    mate(0).start()
    pass_on(distant)
    own_weight.wait()
    by_group(lambda q: beside(q).start())
    arrived(cells.at[pl.ds(2, 2), :, quarter(1 - row, core)], turn_recv)
    mate(1).start()
    arrived(cells.at[pl.ds(1, 1), :, pl.ds(0, 7 * cin)], level_recv)
    mate(2).start()

    @by_group
    def _(q):
        arrived(weights.at[pl.ds(*cuts[1 - q]), pl.ds(0, 7 * cin)], xrecv)
        beside(1 - q).start()

    own_bias.wait()
    cout = weights.shape[2]
    local = 1 + row * 2 + core

    def turn_over(c):
        for tap in range(taps):
            kx, ky, kz = tap // 9, tap // 3 % 3, tap % 3
            turned[c, pl.ds(kz * cout, cout), pl.ds((kx * 3 + ky) * half, half)] = jnp.transpose(
                weights[tap, side(c)]
            )

    def product(c, low, high):
        zero = jnp.zeros((half, wide_z), cells.dtype)
        sides = []
        for kx in range(3):
            for ky in range(3):
                found = [
                    cells[local - 1 + kx, y + ky - 1, side(c)] if 0 <= y + ky - 1 < wide_y else zero
                    for y in range(low, high)
                ]
                sides.append(jnp.concatenate(found, axis=1))
        return jnp.dot(
            turned[c], jnp.concatenate(sides, axis=0), preferred_element_type=jnp.float32
        )

    @pl.when(starts & (bed > 0))
    def _():
        own_first().wait()

    @pl.when(ends & (bed < BEDS - 1))
    def _():
        own_last().wait()

    @pl.when((starts & (bed > 0)) | (ends & (bed < BEDS - 1)))
    def _():
        arrived(cells.at[pl.ds(0, 1), :, pl.ds(0, 15 * cin)], outer_recv)

    turn_over(core)
    for low, high in SPANS:
        total[:, pl.ds(low * wide_z, (high - low) * wide_z)] = product(core, low, high)

    for q in range(2):
        arrived(weights.at[pl.ds(*cuts[q]), side(1 - core)], mrecv.at[q])
    turn_over(1 - core)
    for k in range(3):
        mated(k)

    def edge(k):
        low, high = SPANS[k]
        at = pl.ds(low, high - low)
        return remote(
            hidden.at[0, at], hidden.at[1, at], esend.at[k], erecv.at[k], {"gx": me - 1}
        )

    bias_cells = jnp.transpose(jnp.broadcast_to(bias_row[...], (wide_z, cout)))
    for k, (low, high) in enumerate(SPANS):
        final = total[:, pl.ds(low * wide_z, (high - low) * wide_z)] + product(1 - core, low, high)
        for y in range(low, high):
            part = final[:, (y - low) * wide_z : (y - low + 1) * wide_z]
            hidden[0, y] = jnp.maximum(
                part[cout : 2 * cout]
                + shift_up(part[:cout])
                + shift_down(part[2 * cout :])
                + bias_cells,
                0.0,
            ).astype(jnp.bfloat16)

        @pl.when(me > 0)
        def _(k=k):
            edge(k).start()

    own_fan.wait()
    spread = spreading(wide_z)

    def field(i):
        return lambda y: hidden[i, y]

    def write(pu, low, high):
        fields = ((1, field(0)),) if pu == 0 else ((2, field(0)), (0, field(1)))
        for v, value in upsampled(fields, fan, spread, low, high, wide_y, wide_z):
            decoded[pu, v] = value

    def store(k, pu, low, high):
        at = (pu, pl.ds(2 * low, 2 * (high - low)))
        return pltpu.make_async_copy(decoded.at[at], out.at[at], out_sem.at[k])

    write(0, 0, wide_y)
    store(parts, 0, 0, wide_y).start()

    def sent(at, sem):
        pltpu.make_async_copy(at, at, sem).wait()

    by_group(lambda q: sent(weights.at[pl.ds(*cuts[q]), pl.ds(0, 14 * cin)], wsend))
    for q in range(2):
        beside(q).wait_send()
    sent(cells.at[pl.ds(2, 2), :, pl.ds(0, 7 * cin)], csem_send)
    sent(cells.at[pl.ds(1, 1), :, pl.ds(0, 7 * cin)], level_send)
    fewer = (starts & (bed > 0)) | (ends & (bed < BEDS - 1))

    @pl.when(fewer)
    def _():
        sent(cells.at[pl.ds(1, 1), :, pl.ds(0, 5 * cin)], outer_send)

    @pl.when(jnp.logical_not(fewer))
    def _():
        sent(cells.at[pl.ds(1, 1), :, pl.ds(0, 6 * cin)], outer_send)

    for k in range(3):
        mate(k).wait_send()

    for k, (low, high) in enumerate(SPANS):
        @pl.when(me < count - 1)
        def _(k=k, low=low, high=high):
            arrived(hidden.at[1, pl.ds(low, high - low)], erecv.at[k])

        write(1, *LAST[k])
        store(k, 1, *LAST[k]).start()

    @pl.when(me > 0)
    def _():
        for k in range(parts):
            edge(k).wait_send()

    store(parts, 0, 0, wide_y).wait()
    for k in range(parts):
        store(k, 1, *LAST[k]).wait()


def local_conv(planes, weight, bias, hidden_out):
    wide_y, wide_z = planes.shape[1], planes.shape[3]
    cells = [lambda y, kx=kx: planes[kx, y] for kx in range(3)]
    hidden_out[...] = conv_hidden(cells, wide_y, wide_z, lambda t: weight[t], bias[...])


def spreading(wide_z):
    row = lax.broadcasted_iota(jnp.int32, (2 * wide_z, 2 * wide_z), 0)
    col = lax.broadcasted_iota(jnp.int32, (2 * wide_z, 2 * wide_z), 1)
    return jnp.where(
        col == jnp.where(row < wide_z, 2 * row, 2 * (row - wide_z) + 1), 1.0, 0.0
    ).astype(jnp.bfloat16)


def upsampled(fields, tconv, spread, low, high, wide_y, wide_z):
    cup, cout = tconv.shape[1], tconv.shape[2]
    zero = jnp.zeros((cout, wide_z), jnp.bfloat16)
    found = []
    for pv in range(2):
        left, right = [], []
        for kx, field in fields:
            for ky, shift in (((1, 0),), ((2, 0), (0, 1)))[pv]:
                tap = kx * 9 + ky * 3
                left.append(tconv[tap : tap + 3].reshape(3 * cup, cout))
                right.append(
                    jnp.concatenate(
                        [
                            field(y + shift) if y + shift < wide_y else zero
                            for y in range(low, high)
                        ],
                        axis=1,
                    )
                )
        product = jnp.dot(
            jnp.concatenate(left, axis=1), jnp.concatenate(right, axis=0),
            preferred_element_type=jnp.float32,
        )
        pairs = []
        for i in range(high - low):
            part = product[:, i * wide_z : (i + 1) * wide_z]
            even = part[cup : 2 * cup]
            odd = part[2 * cup :] + shift_down(part[:cup])
            pairs.append(jnp.concatenate([even, odd], axis=1).astype(jnp.bfloat16))
        mixed = jnp.dot(
            jnp.concatenate(pairs, axis=0), spread, preferred_element_type=jnp.float32
        ).astype(jnp.bfloat16)
        for i in range(high - low):
            found.append((2 * (low + i) + pv, mixed[i * cup : (i + 1) * cup]))
    return found


def transposed(hidden, tconv, out):
    wide_y, wide_z = out.shape[1] // 2, out.shape[3] // 2
    spread = spreading(wide_z)

    def field(i):
        return lambda y: hidden[i, y]

    for pu in range(2):
        fields = ((1, field(0)),) if pu == 0 else ((2, field(0)), (0, field(1)))
        for v, value in upsampled(fields, tconv, spread, 0, wide_y, wide_y, wide_z):
            out[pu, v] = value


def native_hidden(volume, conv_weight, bias):
    count = lax.axis_size("gx")
    forward = [(i, i + 1) for i in range(count - 1)]
    backward = [(i + 1, i) for i in range(count - 1)]
    local = lax.all_to_all(volume, "gx", split_axis=0, concat_axis=1, tiled=True)
    weight = lax.all_gather(conv_weight, "gx", axis=0, tiled=True)
    rows = local.shape[0]
    low = lax.ppermute(local[rows - 1 :], "gx", forward)
    high = lax.ppermute(local[:1], "gx", backward)
    planes = jnp.transpose(jnp.concatenate([low, local, high], axis=0), (0, 2, 1, 3))
    weight = jnp.transpose(weight, (1, 0, 2))
    cout = weight.shape[2]
    shape = jax.ShapeDtypeStruct((cout, planes.shape[1] * planes.shape[3]), jnp.bfloat16)
    conv = pl.pallas_call(
        local_conv, out_shape=shape, in_specs=[VMEM] * 3, out_specs=VMEM,
        compiler_params=pltpu.CompilerParams(vmem_limit_bytes=40 << 20),
    )
    hidden = [conv(planes[r : r + 3], weight, bias) for r in range(rows)]
    hidden.append(lax.ppermute(hidden[0], "gx", backward))
    wide_y, wide_z = volume.shape[2], volume.shape[3]
    hidden = [
        jnp.transpose(plane.reshape(cout, wide_y, wide_z), (1, 0, 2)) for plane in hidden
    ]
    return [jnp.stack(hidden[r : r + 2]) for r in range(rows)]


def remote_decoded(volume, conv_weight, bias, tconv_weight):
    count = lax.axis_size("gx")
    cells = jnp.transpose(volume, (0, 2, 1, 3))
    weight = jnp.transpose(conv_weight, (1, 0, 2))
    taps, cin, cout = weight.shape
    wide_y, wide_z = cells.shape[1], cells.shape[3]
    wide = count * cin
    chips = count // 2
    parts = len(SPANS)
    dma = pltpu.SemaphoreType.DMA
    cup = tconv_weight.shape[1]
    shape = (2, 2 * wide_y, cup, 2 * wide_z)
    return pl.pallas_call(
        exchange_conv,
        out_shape=jax.ShapeDtypeStruct(shape, jnp.bfloat16),
        in_specs=[HBM, HBM, HBM, HBM],
        out_specs=HBM,
        scratch_shapes=[
            pltpu.VMEM((6, wide_y, wide, wide_z), jnp.bfloat16),
            pltpu.VMEM((taps, wide, cout), jnp.bfloat16),
            pltpu.VMEM((2, 3 * cout, 9 * wide // 2), jnp.bfloat16),
            pltpu.VMEM((3 * cout, wide_y * wide_z), jnp.float32),
            pltpu.VMEM((2, wide_y, cout, wide_z), jnp.bfloat16),
            pltpu.VMEM((1, cout), jnp.float32),
            pltpu.VMEM(tconv_weight.shape, jnp.bfloat16),
            pltpu.VMEM(shape, jnp.bfloat16),
            dma((parts + 1,)),
            dma((5,)),
            dma(()), dma((BEDS,)), dma(()), dma(()), dma(()), dma(()), dma(()),
            dma((3,)), dma((3,)),
            dma(()), dma((chips,)), dma(()), dma((2,)), dma((2,)),
            dma((parts,)), dma((parts,)),
            pltpu.SemaphoreType.REGULAR((4,)),
        ],
        compiler_params=pltpu.CompilerParams(
            collective_id=0, has_side_effects=True, vmem_limit_bytes=60 << 20
        ),
    )(cells, weight, bias.reshape(1, cout), tconv_weight)


def per_device(volume, conv_weight, conv_bias, tconv_weight):
    count = lax.axis_size("gx")
    rows = volume.shape[0] // count
    bias = conv_bias[:, None]
    suited = (
        rows == 1 and count == 16 and lax.axis_size("groups") == 2
        and volume.shape[1] % 16 == 0 and volume.shape[2] == SPANS[-1][1]
    )
    if suited:
        out = remote_decoded(volume, conv_weight, bias, tconv_weight)
        return jnp.transpose(out, (0, 2, 1, 3))
    cup = tconv_weight.shape[1]
    shape = jax.ShapeDtypeStruct(
        (2, 2 * volume.shape[2], cup, 2 * volume.shape[3]), jnp.bfloat16
    )
    tconv = pl.pallas_call(
        transposed, out_shape=shape, in_specs=[VMEM] * 2, out_specs=VMEM,
        compiler_params=pltpu.CompilerParams(vmem_limit_bytes=40 << 20),
    )
    hidden = native_hidden(volume, conv_weight, bias)
    out = jnp.concatenate([tconv(planes, tconv_weight) for planes in hidden], axis=0)
    return jnp.transpose(out, (0, 2, 1, 3))


def solution(mesh):
    return jax.shard_map(
        per_device,
        mesh=mesh,
        in_specs=(P("groups", "gx", None, None), P("gx", None, None), P(), P()),
        out_specs=P(("groups", "gx"), None, None, None),
        check_vma=False,
    )
```

```python
import jax
import jax.numpy as jnp
from jax import lax
from jax.experimental import pallas as pl
from jax.experimental.pallas import tpu as pltpu
from jax.sharding import PartitionSpec as P

MESH = pl.DeviceIdType.MESH
VMEM = pl.BlockSpec(memory_space=pltpu.VMEM)
HBM = pl.BlockSpec(memory_space=pltpu.HBM)


def shift_up(block):
    lane = lax.broadcasted_iota(jnp.int32, block.shape, 1)
    return jnp.where(lane == 0, 0.0, pltpu.roll(block, 1, axis=1))


def shift_down(block):
    size = block.shape[1]
    lane = lax.broadcasted_iota(jnp.int32, block.shape, 1)
    return jnp.where(lane == size - 1, 0.0, pltpu.roll(block, size - 1, axis=1))


def conv_hidden(planes, wide_y, wide_z, tap, bias, first=0, span=None):
    span = span or wide_y
    zero = jnp.zeros_like(planes[0](0))
    total = None
    for kx in range(3):
        padded = jnp.concatenate(
            [zero] + [planes[kx](y) for y in range(wide_y)] + [zero], axis=1
        )
        for ky in range(3):
            weight = jnp.concatenate([tap(kx * 9 + ky * 3 + kz) for kz in range(3)], axis=1)
            cells = padded[:, (ky + first) * wide_z : (ky + first + span) * wide_z]
            term = lax.dot_general(
                weight, cells, (((0,), (0,)), ((), ())), preferred_element_type=jnp.float32
            )
            total = term if total is None else total + term
    cout = total.shape[0] // 3
    rows = []
    for y in range(span):
        part = total[:, y * wide_z : (y + 1) * wide_z]
        rows.append(
            part[cout : 2 * cout]
            + shift_up(part[:cout])
            + shift_down(part[2 * cout :])
            + bias
        )
    return jnp.maximum(jnp.concatenate(rows, axis=1), 0.0).astype(jnp.bfloat16)


BEDS = 4
SPANS = ((0, 3), (3, 5), (5, 6))
LAST = ((0, 2), (2, 4), (4, 6))


def exchange_conv(volume, weight, bias, tconv, out, cells, weights, turned, total, hidden, bias_row,
                  fan,
                  entry_sem, csem_send, centre_recv, turn_recv, level_send, level_recv, outer_send,
                  outer_recv, csend, crecv, wsend, wrecv, xrecv, msend, mrecv, esend, erecv, known):
    me = lax.axis_index("gx")
    count = lax.axis_size("gx")
    group = lax.axis_index("groups")
    bed, row, core = me // 4, (me // 2) % 2, me % 2
    partner = me + 1 - 2 * core
    wide_y, wide_z = volume.shape[1], volume.shape[3]
    cin = volume.shape[2]
    half = 2 * BEDS * cin
    parts = len(SPANS)
    starts = (row == 0) & (core == 0)
    ends = (row == 1) & (core == 1)

    @pl.when(me == 0)
    def _():
        cells[0] = jnp.zeros(cells.shape[1:], cells.dtype)

    @pl.when(me == count - 1)
    def _():
        cells[5] = jnp.zeros(cells.shape[1:], cells.dtype)
        hidden[1] = jnp.zeros(hidden.shape[1:], hidden.dtype)

    def remote(src, dst, send, recv, target):
        return pltpu.make_async_remote_copy(
            src_ref=src, dst_ref=dst, send_sem=send, recv_sem=recv,
            device_id=target, device_id_type=MESH,
        )

    def arrived(at, sem):
        pltpu.make_async_copy(at, at, sem).wait()

    def index(b, r, c):
        return b * 4 + r * 2 + c

    def slot(b, r, c):
        return pl.ds(pl.multiple_of(((c * 2 + r) * BEDS + b) * cin, cin), cin)

    def other(b, k):
        return (b // 2 + k // 2) % 2 * 2 + (b % 2 + k % 2) % 2

    own = slot(bed, row, core)
    own_cells = pltpu.make_async_copy(
        volume.at[pl.ds(4 * bed, 4)], cells.at[pl.ds(1, 4), :, own], entry_sem.at[0]
    )
    own_weight = pltpu.make_async_copy(weight, weights.at[:, own], entry_sem.at[1])
    own_bias = pltpu.make_async_copy(bias, bias_row, entry_sem.at[2])

    def own_first():
        return pltpu.make_async_copy(
            volume.at[pl.ds(4 * bed - 1, 1)], cells.at[pl.ds(0, 1), :, own], entry_sem.at[3]
        )

    def own_last():
        return pltpu.make_async_copy(
            volume.at[pl.ds(4 * bed + 4, 1)], cells.at[pl.ds(5, 1), :, own], entry_sem.at[3]
        )

    own_cells.start()
    own_weight.start()
    own_bias.start()
    own_fan = pltpu.make_async_copy(tconv, fan, entry_sem.at[4])
    own_fan.start()

    @pl.when(starts & (bed > 0))
    def _():
        own_first().start()

    @pl.when(ends & (bed < BEDS - 1))
    def _():
        own_last().start()

    barrier = pltpu.get_barrier_semaphore()
    reached = (bed > 0).astype(jnp.int32) + (bed < BEDS - 1).astype(jnp.int32) + 2

    def greet(sem):
        def call(target):
            pl.semaphore_signal(sem, inc=1, device_id={"gx": target}, device_id_type=MESH)

        pl.when(bed > 0)(lambda: call(me - 4))
        pl.when(bed < BEDS - 1)(lambda: call(me + 4))
        call(index(bed, 1 - row, core))
        call(partner)

    greet(barrier)
    pl.semaphore_signal(barrier, inc=1, device_id={"groups": 1 - group}, device_id_type=MESH)
    pl.semaphore_wait(barrier, reached + 1)

    def widen(k):
        greet(known.at[k])
        pl.semaphore_wait(known.at[k], reached)

    def centre(b):
        return remote(
            volume.at[pl.ds(4 * b + 1, 2)], cells.at[pl.ds(2, 2), :, own], csem_send,
            centre_recv.at[bed], {"gx": index(b, row, core)},
        )

    def turn(b):
        at = cells.at[pl.ds(2, 2), :, slot(b, row, core)]
        src = volume.at[pl.ds(4 * bed + 1, 2)] if b is bed else at
        return remote(src, at, csem_send, turn_recv, {"gx": index(bed, 1 - row, core)})

    def level(b, plane, near_plane, r):
        return remote(
            volume.at[pl.ds(4 * b + plane, 1)], cells.at[pl.ds(near_plane, 1), :, own], level_send,
            level_recv, {"gx": index(b, r, core)},
        )

    def outer(b, plane, near_plane, r):
        return remote(
            volume.at[pl.ds(4 * b + plane, 1)], cells.at[pl.ds(near_plane, 1), :, own], outer_send,
            outer_recv, {"gx": index(b, r, r)},
        )

    taps = weights.shape[0]
    cuts = ((0, (taps + 1) // 2), ((taps + 1) // 2, taps // 2))

    def shard(b, r, c, q):
        return weights.at[pl.ds(*cuts[q]), slot(b, r, c)]

    def direct(q, b, r):
        return remote(
            weight.at[pl.ds(*cuts[q])], shard(bed, row, core, q), wsend, wrecv.at[bed * 2 + row],
            {"gx": index(b, r, core)},
        )

    def relay(q, b, r):
        at = shard(other(bed, 2), row, core, q)
        return remote(
            at, at, wsend, wrecv.at[other(bed, 2) * 2 + row], {"gx": index(b, r, core)}
        )

    def across(q, b, r):
        at = shard(b, r, core, q)
        return remote(at, at, wsend, xrecv, {"groups": 1 - group})

    def side(c):
        return pl.ds(pl.multiple_of(c * half, half), half)

    def beside(q):
        at = weights.at[pl.ds(*cuts[q]), side(core)]
        return remote(at, at, msend.at[q], mrecv.at[q], {"gx": partner})

    near = [(other(bed, 1), row), (other(bed, 1), 1 - row), (bed, 1 - row)]
    mirror = (other(bed, 2), row)
    distant = [(other(bed, 3), row), (other(bed, 3), 1 - row), (other(bed, 2), 1 - row)]

    def by_group(body):
        for g in range(2):
            pl.when(group == g)(lambda g=g: body(g))

    def take(q, b, r):
        arrived(shard(b, r, core, q), wrecv.at[b * 2 + r])

    def pass_on(places):
        def body(q):
            for b, r in places:
                take(q, b, r)
                across(q, b, r).start()

        by_group(body)

    @by_group
    def _(q):
        direct(q, *near[0]).start()
        direct(q, *near[2]).start()

    turn(bed).start()

    def centres(distance):
        for b in range(BEDS):
            pl.when(jnp.abs(bed - b) == distance)(lambda b=b: centre(b).start())

    centres(1)
    widen(0)

    @by_group
    def _(q):
        direct(q, *mirror).start()
        direct(q, *near[1]).start()

    centres(2)
    widen(1)
    centres(3)
    widen(2)
    widen(3)
    order = [other(bed, k) for k in (2, 3, 1)]

    @by_group
    def _(q):
        take(q, *mirror)
        for b, r in near:
            relay(q, b, r).start()
        across(q, *mirror).start()

    for b in order + [bed]:
        pl.when(index(b, 1, core) != me)(lambda b=b: level(b, 3, 4, 1).start())
    for b in order + [bed]:
        pl.when(index(b, 0, core) != me)(lambda b=b: level(b, 0, 1, 0).start())
    for b in order + [bed]:
        pl.when((index(b, 0, 0) != me) & (b > 0))(lambda b=b: outer(b, -1, 0, 0).start())
    for b in order + [bed]:
        pl.when((index(b, 1, 1) != me) & (b < BEDS - 1))(lambda b=b: outer(b, 4, 5, 1).start())

    pass_on(near)
    for b in order[::-1]:
        arrived(cells.at[pl.ds(2, 2), :, slot(b, row, core)], centre_recv.at[b])
        turn(b).start()
    own_cells.wait()

    def quarter(r, c):
        return pl.ds(pl.multiple_of((c * 2 + r) * BEDS * cin, BEDS * cin), BEDS * cin)

    def mate(k):
        if k < 2:
            at = cells.at[pl.ds(2, 2), :, quarter(row if k == 0 else 1 - row, core)]
        else:
            at = cells.at[pl.ds(1 + 3 * row, 1), :, side(core)]
        return remote(at, at, csend.at[k], crecv.at[k], {"gx": partner})

    def mated(k):
        if k < 2:
            at = cells.at[pl.ds(2, 2), :, quarter(row if k == 0 else 1 - row, 1 - core)]
        else:
            at = cells.at[pl.ds(1 + 3 * row, 1), :, side(1 - core)]
        arrived(at, crecv.at[k])

    mate(0).start()
    pass_on(distant)
    own_weight.wait()
    by_group(lambda q: beside(q).start())
    arrived(cells.at[pl.ds(2, 2), :, quarter(1 - row, core)], turn_recv)
    mate(1).start()
    arrived(cells.at[pl.ds(1, 1), :, pl.ds(0, 7 * cin)], level_recv)
    mate(2).start()

    @by_group
    def _(q):
        arrived(weights.at[pl.ds(*cuts[1 - q]), pl.ds(0, 7 * cin)], xrecv)
        beside(1 - q).start()

    own_bias.wait()
    cout = weights.shape[2]
    local = 1 + row * 2 + core

    def turn_over(c):
        for tap in range(taps):
            kx, ky, kz = tap // 9, tap // 3 % 3, tap % 3
            turned[c, pl.ds(kz * cout, cout), pl.ds((kx * 3 + ky) * half, half)] = jnp.transpose(
                weights[tap, side(c)]
            )

    def product(c, low, high):
        zero = jnp.zeros((half, wide_z), cells.dtype)
        sides = []
        for kx in range(3):
            for ky in range(3):
                found = [
                    cells[local - 1 + kx, y + ky - 1, side(c)] if 0 <= y + ky - 1 < wide_y else zero
                    for y in range(low, high)
                ]
                sides.append(jnp.concatenate(found, axis=1))
        return jnp.dot(
            turned[c], jnp.concatenate(sides, axis=0), preferred_element_type=jnp.float32
        )

    @pl.when(starts & (bed > 0))
    def _():
        own_first().wait()

    @pl.when(ends & (bed < BEDS - 1))
    def _():
        own_last().wait()

    @pl.when((starts & (bed > 0)) | (ends & (bed < BEDS - 1)))
    def _():
        arrived(cells.at[pl.ds(0, 1), :, pl.ds(0, 15 * cin)], outer_recv)

    turn_over(core)
    for low, high in SPANS:
        total[:, pl.ds(low * wide_z, (high - low) * wide_z)] = product(core, low, high)

    for q in range(2):
        arrived(weights.at[pl.ds(*cuts[q]), side(1 - core)], mrecv.at[q])
    turn_over(1 - core)
    for k in range(3):
        mated(k)

    def edge(k):
        low, high = SPANS[k]
        at = pl.ds(low, high - low)
        return remote(
            hidden.at[0, at], hidden.at[1, at], esend.at[k], erecv.at[k], {"gx": me - 1}
        )

    bias_cells = jnp.transpose(jnp.broadcast_to(bias_row[...], (wide_z, cout)))
    for k, (low, high) in enumerate(SPANS):
        final = total[:, pl.ds(low * wide_z, (high - low) * wide_z)] + product(1 - core, low, high)
        for y in range(low, high):
            part = final[:, (y - low) * wide_z : (y - low + 1) * wide_z]
            hidden[0, y] = jnp.maximum(
                part[cout : 2 * cout]
                + shift_up(part[:cout])
                + shift_down(part[2 * cout :])
                + bias_cells,
                0.0,
            ).astype(jnp.bfloat16)

        @pl.when(me > 0)
        def _(k=k):
            edge(k).start()

    own_fan.wait()
    spread = spreading(wide_z)

    def field(i):
        return lambda y: hidden[i, y]

    def write(pu, low, high):
        fields = ((1, field(0)),) if pu == 0 else ((2, field(0)), (0, field(1)))
        for v, value in upsampled(fields, fan, spread, low, high, wide_y, wide_z):
            out[pu, v] = value

    write(0, 0, wide_y)

    def sent(at, sem):
        pltpu.make_async_copy(at, at, sem).wait()

    by_group(lambda q: sent(weights.at[pl.ds(*cuts[q]), pl.ds(0, 14 * cin)], wsend))
    for q in range(2):
        beside(q).wait_send()
    sent(cells.at[pl.ds(2, 2), :, pl.ds(0, 7 * cin)], csem_send)
    sent(cells.at[pl.ds(1, 1), :, pl.ds(0, 7 * cin)], level_send)
    fewer = (starts & (bed > 0)) | (ends & (bed < BEDS - 1))

    @pl.when(fewer)
    def _():
        sent(cells.at[pl.ds(1, 1), :, pl.ds(0, 5 * cin)], outer_send)

    @pl.when(jnp.logical_not(fewer))
    def _():
        sent(cells.at[pl.ds(1, 1), :, pl.ds(0, 6 * cin)], outer_send)

    for k in range(3):
        mate(k).wait_send()

    for k, (low, high) in enumerate(SPANS):
        @pl.when(me < count - 1)
        def _(k=k, low=low, high=high):
            arrived(hidden.at[1, pl.ds(low, high - low)], erecv.at[k])

        write(1, *LAST[k])

    @pl.when(me > 0)
    def _():
        for k in range(parts):
            edge(k).wait_send()


def local_conv(planes, weight, bias, hidden_out):
    wide_y, wide_z = planes.shape[1], planes.shape[3]
    cells = [lambda y, kx=kx: planes[kx, y] for kx in range(3)]
    hidden_out[...] = conv_hidden(cells, wide_y, wide_z, lambda t: weight[t], bias[...])


def spreading(wide_z):
    row = lax.broadcasted_iota(jnp.int32, (2 * wide_z, 2 * wide_z), 0)
    col = lax.broadcasted_iota(jnp.int32, (2 * wide_z, 2 * wide_z), 1)
    return jnp.where(
        col == jnp.where(row < wide_z, 2 * row, 2 * (row - wide_z) + 1), 1.0, 0.0
    ).astype(jnp.bfloat16)


def upsampled(fields, tconv, spread, low, high, wide_y, wide_z):
    cup, cout = tconv.shape[1], tconv.shape[2]
    zero = jnp.zeros((cout, wide_z), jnp.bfloat16)
    found = []
    for pv in range(2):
        left, right = [], []
        for kx, field in fields:
            for ky, shift in (((1, 0),), ((2, 0), (0, 1)))[pv]:
                tap = kx * 9 + ky * 3
                left.append(tconv[tap : tap + 3].reshape(3 * cup, cout))
                right.append(
                    jnp.concatenate(
                        [
                            field(y + shift) if y + shift < wide_y else zero
                            for y in range(low, high)
                        ],
                        axis=1,
                    )
                )
        product = jnp.dot(
            jnp.concatenate(left, axis=1), jnp.concatenate(right, axis=0),
            preferred_element_type=jnp.float32,
        )
        pairs = []
        for i in range(high - low):
            part = product[:, i * wide_z : (i + 1) * wide_z]
            even = part[cup : 2 * cup]
            odd = part[2 * cup :] + shift_down(part[:cup])
            pairs.append(jnp.concatenate([even, odd], axis=1).astype(jnp.bfloat16))
        mixed = jnp.dot(
            jnp.concatenate(pairs, axis=0), spread, preferred_element_type=jnp.float32
        ).astype(jnp.bfloat16)
        for i in range(high - low):
            found.append((2 * (low + i) + pv, mixed[i * cup : (i + 1) * cup]))
    return found


def transposed(hidden, tconv, out):
    wide_y, wide_z = out.shape[1] // 2, out.shape[3] // 2
    spread = spreading(wide_z)

    def field(i):
        return lambda y: hidden[i, y]

    for pu in range(2):
        fields = ((1, field(0)),) if pu == 0 else ((2, field(0)), (0, field(1)))
        for v, value in upsampled(fields, tconv, spread, 0, wide_y, wide_y, wide_z):
            out[pu, v] = value


def native_hidden(volume, conv_weight, bias):
    count = lax.axis_size("gx")
    forward = [(i, i + 1) for i in range(count - 1)]
    backward = [(i + 1, i) for i in range(count - 1)]
    local = lax.all_to_all(volume, "gx", split_axis=0, concat_axis=1, tiled=True)
    weight = lax.all_gather(conv_weight, "gx", axis=0, tiled=True)
    rows = local.shape[0]
    low = lax.ppermute(local[rows - 1 :], "gx", forward)
    high = lax.ppermute(local[:1], "gx", backward)
    planes = jnp.transpose(jnp.concatenate([low, local, high], axis=0), (0, 2, 1, 3))
    weight = jnp.transpose(weight, (1, 0, 2))
    cout = weight.shape[2]
    shape = jax.ShapeDtypeStruct((cout, planes.shape[1] * planes.shape[3]), jnp.bfloat16)
    conv = pl.pallas_call(
        local_conv, out_shape=shape, in_specs=[VMEM] * 3, out_specs=VMEM,
        compiler_params=pltpu.CompilerParams(vmem_limit_bytes=40 << 20),
    )
    hidden = [conv(planes[r : r + 3], weight, bias) for r in range(rows)]
    hidden.append(lax.ppermute(hidden[0], "gx", backward))
    wide_y, wide_z = volume.shape[2], volume.shape[3]
    hidden = [
        jnp.transpose(plane.reshape(cout, wide_y, wide_z), (1, 0, 2)) for plane in hidden
    ]
    return [jnp.stack(hidden[r : r + 2]) for r in range(rows)]


def remote_decoded(volume, conv_weight, bias, tconv_weight):
    count = lax.axis_size("gx")
    cells = jnp.transpose(volume, (0, 2, 1, 3))
    weight = jnp.transpose(conv_weight, (1, 0, 2))
    taps, cin, cout = weight.shape
    wide_y, wide_z = cells.shape[1], cells.shape[3]
    wide = count * cin
    chips = count // 2
    parts = len(SPANS)
    dma = pltpu.SemaphoreType.DMA
    cup = tconv_weight.shape[1]
    shape = (2, 2 * wide_y, cup, 2 * wide_z)
    return pl.pallas_call(
        exchange_conv,
        out_shape=pltpu.VMEM(shape, jnp.bfloat16),
        in_specs=[HBM, HBM, HBM, HBM],
        out_specs=VMEM,
        scratch_shapes=[
            pltpu.VMEM((6, wide_y, wide, wide_z), jnp.bfloat16),
            pltpu.VMEM((taps, wide, cout), jnp.bfloat16),
            pltpu.VMEM((2, 3 * cout, 9 * wide // 2), jnp.bfloat16),
            pltpu.VMEM((3 * cout, wide_y * wide_z), jnp.float32),
            pltpu.VMEM((2, wide_y, cout, wide_z), jnp.bfloat16),
            pltpu.VMEM((1, cout), jnp.float32),
            pltpu.VMEM(tconv_weight.shape, jnp.bfloat16),
            dma((5,)),
            dma(()), dma((BEDS,)), dma(()), dma(()), dma(()), dma(()), dma(()),
            dma((3,)), dma((3,)),
            dma(()), dma((chips,)), dma(()), dma((2,)), dma((2,)),
            dma((parts,)), dma((parts,)),
            pltpu.SemaphoreType.REGULAR((4,)),
        ],
        compiler_params=pltpu.CompilerParams(
            collective_id=0, has_side_effects=True, vmem_limit_bytes=44 << 20
        ),
    )(*(
        pltpu.with_memory_space_constraint(given, pltpu.HBM)
        for given in (cells, weight, bias.reshape(1, cout), tconv_weight)
    ))


def per_device(volume, conv_weight, conv_bias, tconv_weight):
    count = lax.axis_size("gx")
    rows = volume.shape[0] // count
    bias = conv_bias[:, None]
    suited = (
        rows == 1 and count == 16 and lax.axis_size("groups") == 2
        and volume.shape[1] % 16 == 0 and volume.shape[2] == SPANS[-1][1]
    )
    if suited:
        out = remote_decoded(volume, conv_weight, bias, tconv_weight)
        return jnp.transpose(out, (0, 2, 1, 3))
    cup = tconv_weight.shape[1]
    shape = jax.ShapeDtypeStruct(
        (2, 2 * volume.shape[2], cup, 2 * volume.shape[3]), jnp.bfloat16
    )
    tconv = pl.pallas_call(
        transposed, out_shape=shape, in_specs=[VMEM] * 2, out_specs=VMEM,
        compiler_params=pltpu.CompilerParams(vmem_limit_bytes=40 << 20),
    )
    hidden = native_hidden(volume, conv_weight, bias)
    out = jnp.concatenate([tconv(planes, tconv_weight) for planes in hidden], axis=0)
    return jnp.transpose(out, (0, 2, 1, 3))


def solution(mesh):
    return jax.shard_map(
        per_device,
        mesh=mesh,
        in_specs=(P("groups", "gx", None, None), P("gx", None, None), P(), P()),
        out_specs=P(("groups", "gx"), None, None, None),
        check_vma=False,
    )
```

```python
import jax
import jax.numpy as jnp
from jax import lax
from jax.experimental import pallas as pl
from jax.experimental.pallas import tpu as pltpu
from jax.sharding import PartitionSpec as P

MESH = pl.DeviceIdType.MESH
VMEM = pl.BlockSpec(memory_space=pltpu.VMEM)
HBM = pl.BlockSpec(memory_space=pltpu.HBM)


def shift_up(block):
    lane = lax.broadcasted_iota(jnp.int32, block.shape, 1)
    return jnp.where(lane == 0, 0.0, pltpu.roll(block, 1, axis=1))


def shift_down(block):
    size = block.shape[1]
    lane = lax.broadcasted_iota(jnp.int32, block.shape, 1)
    return jnp.where(lane == size - 1, 0.0, pltpu.roll(block, size - 1, axis=1))


def conv_hidden(planes, wide_y, wide_z, tap, bias, first=0, span=None):
    span = span or wide_y
    zero = jnp.zeros_like(planes[0](0))
    total = None
    for kx in range(3):
        padded = jnp.concatenate(
            [zero] + [planes[kx](y) for y in range(wide_y)] + [zero], axis=1
        )
        for ky in range(3):
            weight = jnp.concatenate([tap(kx * 9 + ky * 3 + kz) for kz in range(3)], axis=1)
            cells = padded[:, (ky + first) * wide_z : (ky + first + span) * wide_z]
            term = lax.dot_general(
                weight, cells, (((0,), (0,)), ((), ())), preferred_element_type=jnp.float32
            )
            total = term if total is None else total + term
    cout = total.shape[0] // 3
    rows = []
    for y in range(span):
        part = total[:, y * wide_z : (y + 1) * wide_z]
        rows.append(
            part[cout : 2 * cout]
            + shift_up(part[:cout])
            + shift_down(part[2 * cout :])
            + bias
        )
    return jnp.maximum(jnp.concatenate(rows, axis=1), 0.0).astype(jnp.bfloat16)


BEDS = 4
SPANS = ((0, 3), (3, 5), (5, 6))
LAST = ((0, 2), (2, 4), (4, 6))


def exchange_conv(volume, weight, bias, tconv, out, cells, weights, turned, total, hidden, bias_row,
                  fan,
                  entry_sem, csem_send, centre_recv, turn_recv, level_send, level_recv, outer_send,
                  outer_recv, csend, crecv, wsend, wrecv, xrecv, msend, mrecv, esend, erecv, known):
    me = lax.axis_index("gx")
    count = lax.axis_size("gx")
    group = lax.axis_index("groups")
    bed, row, core = me // 4, (me // 2) % 2, me % 2
    partner = me + 1 - 2 * core
    wide_y, wide_z = volume.shape[1], volume.shape[3]
    cin = volume.shape[2]
    half = 2 * BEDS * cin
    parts = len(SPANS)
    starts = (row == 0) & (core == 0)
    ends = (row == 1) & (core == 1)

    @pl.when(me == 0)
    def _():
        cells[0] = jnp.zeros(cells.shape[1:], cells.dtype)

    @pl.when(me == count - 1)
    def _():
        cells[5] = jnp.zeros(cells.shape[1:], cells.dtype)
        hidden[1] = jnp.zeros(hidden.shape[1:], hidden.dtype)

    def remote(src, dst, send, recv, target):
        return pltpu.make_async_remote_copy(
            src_ref=src, dst_ref=dst, send_sem=send, recv_sem=recv,
            device_id=target, device_id_type=MESH,
        )

    def arrived(at, sem):
        pltpu.make_async_copy(at, at, sem).wait()

    def index(b, r, c):
        return b * 4 + r * 2 + c

    def slot(b, r, c):
        return pl.ds(pl.multiple_of(((c * 2 + r) * BEDS + b) * cin, cin), cin)

    def other(b, k):
        return (b // 2 + k // 2) % 2 * 2 + (b % 2 + k % 2) % 2

    own = slot(bed, row, core)
    own_cells = pltpu.make_async_copy(
        volume.at[pl.ds(4 * bed, 4)], cells.at[pl.ds(1, 4), :, own], entry_sem.at[0]
    )
    own_weight = pltpu.make_async_copy(weight, weights.at[:, own], entry_sem.at[1])
    own_bias = pltpu.make_async_copy(bias, bias_row, entry_sem.at[2])

    def own_first():
        return pltpu.make_async_copy(
            volume.at[pl.ds(4 * bed - 1, 1)], cells.at[pl.ds(0, 1), :, own], entry_sem.at[3]
        )

    def own_last():
        return pltpu.make_async_copy(
            volume.at[pl.ds(4 * bed + 4, 1)], cells.at[pl.ds(5, 1), :, own], entry_sem.at[3]
        )

    own_cells.start()
    own_weight.start()
    own_bias.start()
    own_fan = pltpu.make_async_copy(tconv, fan, entry_sem.at[4])
    own_fan.start()

    @pl.when(starts & (bed > 0))
    def _():
        own_first().start()

    @pl.when(ends & (bed < BEDS - 1))
    def _():
        own_last().start()

    barrier = pltpu.get_barrier_semaphore()
    reached = (bed > 0).astype(jnp.int32) + (bed < BEDS - 1).astype(jnp.int32) + 2

    def greet(sem):
        def call(target):
            pl.semaphore_signal(sem, inc=1, device_id={"gx": target}, device_id_type=MESH)

        pl.when(bed > 0)(lambda: call(me - 4))
        pl.when(bed < BEDS - 1)(lambda: call(me + 4))
        call(index(bed, 1 - row, core))
        call(partner)

    greet(barrier)
    pl.semaphore_signal(barrier, inc=1, device_id={"groups": 1 - group}, device_id_type=MESH)
    pl.semaphore_wait(barrier, reached + 1)

    def widen(k):
        greet(known.at[k])
        pl.semaphore_wait(known.at[k], reached)

    def centre(b):
        return remote(
            volume.at[pl.ds(4 * b + 1, 2)], cells.at[pl.ds(2, 2), :, own], csem_send,
            centre_recv.at[bed], {"gx": index(b, row, core)},
        )

    def turn(b):
        at = cells.at[pl.ds(2, 2), :, slot(b, row, core)]
        src = volume.at[pl.ds(4 * bed + 1, 2)] if b is bed else at
        return remote(src, at, csem_send, turn_recv, {"gx": index(bed, 1 - row, core)})

    def level(b, plane, near_plane, r):
        return remote(
            volume.at[pl.ds(4 * b + plane, 1)], cells.at[pl.ds(near_plane, 1), :, own], level_send,
            level_recv, {"gx": index(b, r, core)},
        )

    def outer(b, plane, near_plane, r):
        return remote(
            volume.at[pl.ds(4 * b + plane, 1)], cells.at[pl.ds(near_plane, 1), :, own], outer_send,
            outer_recv, {"gx": index(b, r, r)},
        )

    taps = weights.shape[0]
    cuts = ((0, (taps + 1) // 2), ((taps + 1) // 2, taps // 2))

    fine = [((a, (n + 1) // 2), (a + (n + 1) // 2, n // 2)) for a, n in cuts]

    def shard(b, r, c, q, s=None):
        return weights.at[pl.ds(*(cuts[q] if s is None else fine[q][s])), slot(b, r, c)]

    def direct(q, b, r, s=None):
        return remote(
            weight.at[pl.ds(*(cuts[q] if s is None else fine[q][s]))],
            shard(bed, row, core, q, s), wsend, wrecv.at[s or 0, bed * 2 + row],
            {"gx": index(b, r, core)},
        )

    def relay(q, b, r, s):
        at = shard(other(bed, 2), row, core, q, s)
        return remote(
            at, at, wsend, wrecv.at[s, other(bed, 2) * 2 + row], {"gx": index(b, r, core)}
        )

    def across(q, b, r, s=None):
        at = shard(b, r, core, q, s)
        return remote(at, at, wsend, xrecv, {"groups": 1 - group})

    def side(c):
        return pl.ds(pl.multiple_of(c * half, half), half)

    def beside(q):
        at = weights.at[pl.ds(*cuts[q]), side(core)]
        return remote(at, at, msend.at[q], mrecv.at[q], {"gx": partner})

    near = [(other(bed, 1), row), (other(bed, 1), 1 - row), (bed, 1 - row)]
    mirror = (other(bed, 2), row)
    distant = [(other(bed, 3), row), (other(bed, 3), 1 - row), (other(bed, 2), 1 - row)]

    def by_group(body):
        for g in range(2):
            pl.when(group == g)(lambda g=g: body(g))

    def take(q, b, r, s=None):
        arrived(shard(b, r, core, q, s), wrecv.at[s or 0, b * 2 + r])

    def pass_on(places, steps):
        def body(q):
            for s in steps:
                for b, r in places:
                    take(q, b, r, s)
                    across(q, b, r, s).start()

        by_group(body)

    @by_group
    def _(q):
        direct(q, *near[0]).start()
        direct(q, *near[2]).start()

    turn(bed).start()

    def centres(distance):
        for b in range(BEDS):
            pl.when(jnp.abs(bed - b) == distance)(lambda b=b: centre(b).start())

    centres(1)
    widen(0)

    @by_group
    def _(q):
        for s in range(2):
            direct(q, *mirror, s).start()
        direct(q, *near[1]).start()

    centres(2)
    widen(1)
    centres(3)
    widen(2)
    widen(3)
    order = [other(bed, k) for k in (2, 3, 1)]

    @by_group
    def _(q):
        for s in range(2):
            take(q, *mirror, s)
            for b, r in near:
                relay(q, b, r, s).start()
            across(q, *mirror, s).start()

    for b in [order[1], order[0], order[2], bed]:
        pl.when(index(b, 1, core) != me)(lambda b=b: level(b, 3, 4, 1).start())
    for b in [order[1], order[0], order[2], bed]:
        pl.when(index(b, 0, core) != me)(lambda b=b: level(b, 0, 1, 0).start())
    for b in [order[1], order[0], order[2], bed]:
        pl.when((index(b, 0, 0) != me) & (b > 0))(lambda b=b: outer(b, -1, 0, 0).start())
    for b in [order[1], order[0], order[2], bed]:
        pl.when((index(b, 1, 1) != me) & (b < BEDS - 1))(lambda b=b: outer(b, 4, 5, 1).start())

    pass_on(near, (None,))
    for b in order[::-1]:
        arrived(cells.at[pl.ds(2, 2), :, slot(b, row, core)], centre_recv.at[b])
        turn(b).start()
    own_cells.wait()

    def quarter(r, c):
        return pl.ds(pl.multiple_of((c * 2 + r) * BEDS * cin, BEDS * cin), BEDS * cin)

    def mate(k):
        if k < 2:
            at = cells.at[pl.ds(2, 2), :, quarter(row if k == 0 else 1 - row, core)]
        else:
            at = cells.at[pl.ds(1 + 3 * row, 1), :, side(core)]
        return remote(at, at, csend.at[k], crecv.at[k], {"gx": partner})

    def mated(k):
        if k < 2:
            at = cells.at[pl.ds(2, 2), :, quarter(row if k == 0 else 1 - row, 1 - core)]
        else:
            at = cells.at[pl.ds(1 + 3 * row, 1), :, side(1 - core)]
        arrived(at, crecv.at[k])

    mate(0).start()
    pass_on(distant, range(2))
    own_weight.wait()
    by_group(lambda q: beside(q).start())
    arrived(cells.at[pl.ds(2, 2), :, quarter(1 - row, core)], turn_recv)
    mate(1).start()
    arrived(cells.at[pl.ds(1, 1), :, pl.ds(0, 7 * cin)], level_recv)
    mate(2).start()

    @by_group
    def _(q):
        arrived(weights.at[pl.ds(*cuts[1 - q]), pl.ds(0, 7 * cin)], xrecv)
        beside(1 - q).start()

    own_bias.wait()
    cout = weights.shape[2]
    local = 1 + row * 2 + core

    def turn_over(c):
        for tap in range(taps):
            kx, ky, kz = tap // 9, tap // 3 % 3, tap % 3
            turned[c, pl.ds(kz * cout, cout), pl.ds((kx * 3 + ky) * half, half)] = jnp.transpose(
                weights[tap, side(c)]
            )

    def product(c, low, high):
        zero = jnp.zeros((half, wide_z), cells.dtype)
        sides = []
        for kx in range(3):
            for ky in range(3):
                found = [
                    cells[local - 1 + kx, y + ky - 1, side(c)] if 0 <= y + ky - 1 < wide_y else zero
                    for y in range(low, high)
                ]
                sides.append(jnp.concatenate(found, axis=1))
        return jnp.dot(
            turned[c], jnp.concatenate(sides, axis=0), preferred_element_type=jnp.float32
        )

    @pl.when(starts & (bed > 0))
    def _():
        own_first().wait()

    @pl.when(ends & (bed < BEDS - 1))
    def _():
        own_last().wait()

    @pl.when((starts & (bed > 0)) | (ends & (bed < BEDS - 1)))
    def _():
        arrived(cells.at[pl.ds(0, 1), :, pl.ds(0, 15 * cin)], outer_recv)

    turn_over(core)
    for low, high in ((0, 2), (2, 4), (4, 6)):
        total[:, pl.ds(low * wide_z, (high - low) * wide_z)] = product(core, low, high)

    for q in range(2):
        arrived(weights.at[pl.ds(*cuts[q]), side(1 - core)], mrecv.at[q])
    turn_over(1 - core)
    for k in range(3):
        mated(k)

    def edge(k):
        low, high = SPANS[k]
        at = pl.ds(low, high - low)
        return remote(
            hidden.at[0, at], hidden.at[1, at], esend.at[k], erecv.at[k], {"gx": me - 1}
        )

    bias_cells = jnp.transpose(jnp.broadcast_to(bias_row[...], (wide_z, cout)))
    for k, (low, high) in enumerate(SPANS):
        final = total[:, pl.ds(low * wide_z, (high - low) * wide_z)] + product(1 - core, low, high)
        for y in range(low, high):
            part = final[:, (y - low) * wide_z : (y - low + 1) * wide_z]
            hidden[0, y] = jnp.maximum(
                part[cout : 2 * cout]
                + shift_up(part[:cout])
                + shift_down(part[2 * cout :])
                + bias_cells,
                0.0,
            ).astype(jnp.bfloat16)

        @pl.when(me > 0)
        def _(k=k):
            edge(k).start()

    own_fan.wait()
    spread = spreading(wide_z)

    def field(i):
        return lambda y: hidden[i, y]

    def write(pu, low, high):
        fields = ((1, field(0)),) if pu == 0 else ((2, field(0)), (0, field(1)))
        for v, value in upsampled(fields, fan, spread, low, high, wide_y, wide_z):
            out[pu, v] = value

    write(0, 0, wide_y)

    def sent(at, sem):
        pltpu.make_async_copy(at, at, sem).wait()

    by_group(lambda q: sent(weights.at[pl.ds(*cuts[q]), pl.ds(0, 14 * cin)], wsend))
    for q in range(2):
        beside(q).wait_send()
    sent(cells.at[pl.ds(2, 2), :, pl.ds(0, 7 * cin)], csem_send)
    sent(cells.at[pl.ds(1, 1), :, pl.ds(0, 7 * cin)], level_send)
    fewer = (starts & (bed > 0)) | (ends & (bed < BEDS - 1))

    @pl.when(fewer)
    def _():
        sent(cells.at[pl.ds(1, 1), :, pl.ds(0, 5 * cin)], outer_send)

    @pl.when(jnp.logical_not(fewer))
    def _():
        sent(cells.at[pl.ds(1, 1), :, pl.ds(0, 6 * cin)], outer_send)

    for k in range(3):
        mate(k).wait_send()

    for k, (low, high) in enumerate(SPANS):
        @pl.when(me < count - 1)
        def _(k=k, low=low, high=high):
            arrived(hidden.at[1, pl.ds(low, high - low)], erecv.at[k])

        write(1, *LAST[k])

    @pl.when(me > 0)
    def _():
        for k in range(parts):
            edge(k).wait_send()


def local_conv(planes, weight, bias, hidden_out):
    wide_y, wide_z = planes.shape[1], planes.shape[3]
    cells = [lambda y, kx=kx: planes[kx, y] for kx in range(3)]
    hidden_out[...] = conv_hidden(cells, wide_y, wide_z, lambda t: weight[t], bias[...])


def spreading(wide_z):
    row = lax.broadcasted_iota(jnp.int32, (2 * wide_z, 2 * wide_z), 0)
    col = lax.broadcasted_iota(jnp.int32, (2 * wide_z, 2 * wide_z), 1)
    return jnp.where(
        col == jnp.where(row < wide_z, 2 * row, 2 * (row - wide_z) + 1), 1.0, 0.0
    ).astype(jnp.bfloat16)


def upsampled(fields, tconv, spread, low, high, wide_y, wide_z):
    cup, cout = tconv.shape[1], tconv.shape[2]
    zero = jnp.zeros((cout, wide_z), jnp.bfloat16)
    found = []
    for pv in range(2):
        left, right = [], []
        for kx, field in fields:
            for ky, shift in (((1, 0),), ((2, 0), (0, 1)))[pv]:
                tap = kx * 9 + ky * 3
                left.append(tconv[tap : tap + 3].reshape(3 * cup, cout))
                right.append(
                    jnp.concatenate(
                        [
                            field(y + shift) if y + shift < wide_y else zero
                            for y in range(low, high)
                        ],
                        axis=1,
                    )
                )
        product = jnp.dot(
            jnp.concatenate(left, axis=1), jnp.concatenate(right, axis=0),
            preferred_element_type=jnp.float32,
        )
        pairs = []
        for i in range(high - low):
            part = product[:, i * wide_z : (i + 1) * wide_z]
            even = part[cup : 2 * cup]
            odd = part[2 * cup :] + shift_down(part[:cup])
            pairs.append(jnp.concatenate([even, odd], axis=1).astype(jnp.bfloat16))
        mixed = jnp.dot(
            jnp.concatenate(pairs, axis=0), spread, preferred_element_type=jnp.float32
        ).astype(jnp.bfloat16)
        for i in range(high - low):
            found.append((2 * (low + i) + pv, mixed[i * cup : (i + 1) * cup]))
    return found


def transposed(hidden, tconv, out):
    wide_y, wide_z = out.shape[1] // 2, out.shape[3] // 2
    spread = spreading(wide_z)

    def field(i):
        return lambda y: hidden[i, y]

    for pu in range(2):
        fields = ((1, field(0)),) if pu == 0 else ((2, field(0)), (0, field(1)))
        for v, value in upsampled(fields, tconv, spread, 0, wide_y, wide_y, wide_z):
            out[pu, v] = value


def native_hidden(volume, conv_weight, bias):
    count = lax.axis_size("gx")
    forward = [(i, i + 1) for i in range(count - 1)]
    backward = [(i + 1, i) for i in range(count - 1)]
    local = lax.all_to_all(volume, "gx", split_axis=0, concat_axis=1, tiled=True)
    weight = lax.all_gather(conv_weight, "gx", axis=0, tiled=True)
    rows = local.shape[0]
    low = lax.ppermute(local[rows - 1 :], "gx", forward)
    high = lax.ppermute(local[:1], "gx", backward)
    planes = jnp.transpose(jnp.concatenate([low, local, high], axis=0), (0, 2, 1, 3))
    weight = jnp.transpose(weight, (1, 0, 2))
    cout = weight.shape[2]
    shape = jax.ShapeDtypeStruct((cout, planes.shape[1] * planes.shape[3]), jnp.bfloat16)
    conv = pl.pallas_call(
        local_conv, out_shape=shape, in_specs=[VMEM] * 3, out_specs=VMEM,
        compiler_params=pltpu.CompilerParams(vmem_limit_bytes=40 << 20),
    )
    hidden = [conv(planes[r : r + 3], weight, bias) for r in range(rows)]
    hidden.append(lax.ppermute(hidden[0], "gx", backward))
    wide_y, wide_z = volume.shape[2], volume.shape[3]
    hidden = [
        jnp.transpose(plane.reshape(cout, wide_y, wide_z), (1, 0, 2)) for plane in hidden
    ]
    return [jnp.stack(hidden[r : r + 2]) for r in range(rows)]


def remote_decoded(volume, conv_weight, bias, tconv_weight):
    count = lax.axis_size("gx")
    cells = jnp.transpose(volume, (0, 2, 1, 3))
    weight = jnp.transpose(conv_weight, (1, 0, 2))
    taps, cin, cout = weight.shape
    wide_y, wide_z = cells.shape[1], cells.shape[3]
    wide = count * cin
    chips = count // 2
    parts = len(SPANS)
    dma = pltpu.SemaphoreType.DMA
    cup = tconv_weight.shape[1]
    shape = (2, 2 * wide_y, cup, 2 * wide_z)
    return pl.pallas_call(
        exchange_conv,
        out_shape=pltpu.VMEM(shape, jnp.bfloat16),
        in_specs=[HBM, HBM, HBM, HBM],
        out_specs=VMEM,
        scratch_shapes=[
            pltpu.VMEM((6, wide_y, wide, wide_z), jnp.bfloat16),
            pltpu.VMEM((taps, wide, cout), jnp.bfloat16),
            pltpu.VMEM((2, 3 * cout, 9 * wide // 2), jnp.bfloat16),
            pltpu.VMEM((3 * cout, wide_y * wide_z), jnp.float32),
            pltpu.VMEM((2, wide_y, cout, wide_z), jnp.bfloat16),
            pltpu.VMEM((1, cout), jnp.float32),
            pltpu.VMEM(tconv_weight.shape, jnp.bfloat16),
            dma((5,)),
            dma(()), dma((BEDS,)), dma(()), dma(()), dma(()), dma(()), dma(()),
            dma((3,)), dma((3,)),
            dma(()), dma((2, chips)), dma(()), dma((2,)), dma((2,)),
            dma((parts,)), dma((parts,)),
            pltpu.SemaphoreType.REGULAR((4,)),
        ],
        compiler_params=pltpu.CompilerParams(
            collective_id=0, has_side_effects=True, vmem_limit_bytes=44 << 20
        ),
    )(*(
        pltpu.with_memory_space_constraint(given, pltpu.HBM)
        for given in (cells, weight, bias.reshape(1, cout), tconv_weight)
    ))


def per_device(volume, conv_weight, conv_bias, tconv_weight):
    count = lax.axis_size("gx")
    rows = volume.shape[0] // count
    bias = conv_bias[:, None]
    suited = (
        rows == 1 and count == 16 and lax.axis_size("groups") == 2
        and volume.shape[1] % 16 == 0 and volume.shape[2] == SPANS[-1][1]
    )
    if suited:
        out = remote_decoded(volume, conv_weight, bias, tconv_weight)
        return jnp.transpose(out, (0, 2, 1, 3))
    cup = tconv_weight.shape[1]
    shape = jax.ShapeDtypeStruct(
        (2, 2 * volume.shape[2], cup, 2 * volume.shape[3]), jnp.bfloat16
    )
    tconv = pl.pallas_call(
        transposed, out_shape=shape, in_specs=[VMEM] * 2, out_specs=VMEM,
        compiler_params=pltpu.CompilerParams(vmem_limit_bytes=40 << 20),
    )
    hidden = native_hidden(volume, conv_weight, bias)
    out = jnp.concatenate([tconv(planes, tconv_weight) for planes in hidden], axis=0)
    return jnp.transpose(out, (0, 2, 1, 3))


def solution(mesh):
    return jax.shard_map(
        per_device,
        mesh=mesh,
        in_specs=(P("groups", "gx", None, None), P("gx", None, None), P(), P()),
        out_specs=P(("groups", "gx"), None, None, None),
        check_vma=False,
    )
```

```python
import jax
import jax.numpy as jnp
from jax import lax
from jax.experimental import pallas as pl
from jax.experimental.pallas import tpu as pltpu
from jax.sharding import PartitionSpec as P

MESH = pl.DeviceIdType.MESH
VMEM = pl.BlockSpec(memory_space=pltpu.VMEM)
HBM = pl.BlockSpec(memory_space=pltpu.HBM)


def shift_up(block):
    lane = lax.broadcasted_iota(jnp.int32, block.shape, 1)
    return jnp.where(lane == 0, 0.0, pltpu.roll(block, 1, axis=1))


def shift_down(block):
    size = block.shape[1]
    lane = lax.broadcasted_iota(jnp.int32, block.shape, 1)
    return jnp.where(lane == size - 1, 0.0, pltpu.roll(block, size - 1, axis=1))


def conv_hidden(planes, wide_y, wide_z, tap, bias, first=0, span=None):
    span = span or wide_y
    zero = jnp.zeros_like(planes[0](0))
    total = None
    for kx in range(3):
        padded = jnp.concatenate(
            [zero] + [planes[kx](y) for y in range(wide_y)] + [zero], axis=1
        )
        for ky in range(3):
            weight = jnp.concatenate([tap(kx * 9 + ky * 3 + kz) for kz in range(3)], axis=1)
            cells = padded[:, (ky + first) * wide_z : (ky + first + span) * wide_z]
            term = lax.dot_general(
                weight, cells, (((0,), (0,)), ((), ())), preferred_element_type=jnp.float32
            )
            total = term if total is None else total + term
    cout = total.shape[0] // 3
    rows = []
    for y in range(span):
        part = total[:, y * wide_z : (y + 1) * wide_z]
        rows.append(
            part[cout : 2 * cout]
            + shift_up(part[:cout])
            + shift_down(part[2 * cout :])
            + bias
        )
    return jnp.maximum(jnp.concatenate(rows, axis=1), 0.0).astype(jnp.bfloat16)


BEDS = 4
SPANS = ((0, 3), (3, 5), (5, 6))
LAST = ((0, 2), (2, 4), (4, 6))


def exchange_conv(volume, weight, bias, tconv, out, cells, weights, turned, total, hidden, bias_row,
                  fan,
                  entry_sem, csem_send, centre_recv, turn_recv, level_send, level_recv, outer_send,
                  outer_recv, csend, crecv, wsend, wrecv, xrecv, msend, mrecv, esend, erecv, known):
    me = lax.axis_index("gx")
    count = lax.axis_size("gx")
    group = lax.axis_index("groups")
    bed, row, core = me // 4, (me // 2) % 2, me % 2
    partner = me + 1 - 2 * core
    wide_y, wide_z = volume.shape[1], volume.shape[3]
    cin = volume.shape[2]
    half = 2 * BEDS * cin
    parts = len(SPANS)
    starts = (row == 0) & (core == 0)
    ends = (row == 1) & (core == 1)

    @pl.when(me == 0)
    def _():
        cells[0] = jnp.zeros(cells.shape[1:], cells.dtype)

    @pl.when(me == count - 1)
    def _():
        cells[5] = jnp.zeros(cells.shape[1:], cells.dtype)
        hidden[1] = jnp.zeros(hidden.shape[1:], hidden.dtype)

    def remote(src, dst, send, recv, target):
        return pltpu.make_async_remote_copy(
            src_ref=src, dst_ref=dst, send_sem=send, recv_sem=recv,
            device_id=target, device_id_type=MESH,
        )

    def arrived(at, sem):
        pltpu.make_async_copy(at, at, sem).wait()

    def index(b, r, c):
        return b * 4 + r * 2 + c

    def slot(b, r, c):
        return pl.ds(pl.multiple_of(((c * 2 + r) * BEDS + b) * cin, cin), cin)

    def other(b, k):
        return (b // 2 + k // 2) % 2 * 2 + (b % 2 + k % 2) % 2

    own = slot(bed, row, core)
    own_cells = pltpu.make_async_copy(
        volume.at[pl.ds(4 * bed, 4)], cells.at[pl.ds(1, 4), :, own], entry_sem.at[0]
    )
    own_weight = pltpu.make_async_copy(weight, weights.at[:, own], entry_sem.at[1])
    own_bias = pltpu.make_async_copy(bias, bias_row, entry_sem.at[2])

    def own_first():
        return pltpu.make_async_copy(
            volume.at[pl.ds(4 * bed - 1, 1)], cells.at[pl.ds(0, 1), :, own], entry_sem.at[3]
        )

    def own_last():
        return pltpu.make_async_copy(
            volume.at[pl.ds(4 * bed + 4, 1)], cells.at[pl.ds(5, 1), :, own], entry_sem.at[3]
        )

    own_cells.start()
    own_weight.start()
    own_bias.start()
    own_fan = pltpu.make_async_copy(tconv, fan, entry_sem.at[4])
    own_fan.start()

    @pl.when(starts & (bed > 0))
    def _():
        own_first().start()

    @pl.when(ends & (bed < BEDS - 1))
    def _():
        own_last().start()

    barrier = pltpu.get_barrier_semaphore()
    reached = (bed > 0).astype(jnp.int32) + (bed < BEDS - 1).astype(jnp.int32) + 2

    def greet(sem):
        def call(target):
            pl.semaphore_signal(sem, inc=1, device_id={"gx": target}, device_id_type=MESH)

        pl.when(bed > 0)(lambda: call(me - 4))
        pl.when(bed < BEDS - 1)(lambda: call(me + 4))
        call(index(bed, 1 - row, core))
        call(partner)

    greet(barrier)
    pl.semaphore_signal(barrier, inc=1, device_id={"groups": 1 - group}, device_id_type=MESH)
    pl.semaphore_wait(barrier, reached + 1)

    def widen(k):
        greet(known.at[k])
        pl.semaphore_wait(known.at[k], reached)

    def centre(b):
        return remote(
            volume.at[pl.ds(4 * b + 1, 2)], cells.at[pl.ds(2, 2), :, own], csem_send,
            centre_recv.at[bed], {"gx": index(b, row, core)},
        )

    def turn(b):
        at = cells.at[pl.ds(2, 2), :, slot(b, row, core)]
        src = volume.at[pl.ds(4 * bed + 1, 2)] if b is bed else at
        return remote(src, at, csem_send, turn_recv, {"gx": index(bed, 1 - row, core)})

    def level(b, plane, near_plane, r):
        return remote(
            volume.at[pl.ds(4 * b + plane, 1)], cells.at[pl.ds(near_plane, 1), :, own], level_send,
            level_recv, {"gx": index(b, r, core)},
        )

    def outer(b, plane, near_plane, r):
        return remote(
            volume.at[pl.ds(4 * b + plane, 1)], cells.at[pl.ds(near_plane, 1), :, own], outer_send,
            outer_recv, {"gx": index(b, r, r)},
        )

    taps = weights.shape[0]
    cuts = ((0, (taps + 1) // 2), ((taps + 1) // 2, taps // 2))

    fine = [((a, (n + 1) // 2), (a + (n + 1) // 2, n // 2)) for a, n in cuts]

    def shard(b, r, c, q, s=None):
        return weights.at[pl.ds(*(cuts[q] if s is None else fine[q][s])), slot(b, r, c)]

    def direct(q, b, r, s=None):
        return remote(
            weight.at[pl.ds(*(cuts[q] if s is None else fine[q][s]))],
            shard(bed, row, core, q, s), wsend, wrecv.at[s or 0, bed * 2 + row],
            {"gx": index(b, r, core)},
        )

    def relay(q, b, r, s):
        at = shard(other(bed, 2), row, core, q, s)
        return remote(
            at, at, wsend, wrecv.at[s, other(bed, 2) * 2 + row], {"gx": index(b, r, core)}
        )

    def across(q, b, r, s=None):
        at = shard(b, r, core, q, s)
        return remote(at, at, wsend, xrecv, {"groups": 1 - group})

    def side(c):
        return pl.ds(pl.multiple_of(c * half, half), half)

    def beside(q):
        at = weights.at[pl.ds(*cuts[q]), side(core)]
        return remote(at, at, msend.at[q], mrecv.at[q], {"gx": partner})

    near = [(other(bed, 1), row), (other(bed, 1), 1 - row), (bed, 1 - row)]
    mirror = (other(bed, 2), row)
    distant = [(other(bed, 3), row), (other(bed, 3), 1 - row), (other(bed, 2), 1 - row)]

    def by_group(body):
        for g in range(2):
            pl.when(group == g)(lambda g=g: body(g))

    def take(q, b, r, s=None):
        arrived(shard(b, r, core, q, s), wrecv.at[s or 0, b * 2 + r])

    def pass_on(places, steps):
        def body(q):
            for s in steps:
                for b, r in places:
                    take(q, b, r, s)
                    across(q, b, r, s).start()

        by_group(body)

    @by_group
    def _(q):
        for s in range(2):
            direct(q, *near[0], s).start()
            direct(q, *near[2], s).start()

    turn(bed).start()

    def centres(distance):
        for b in range(BEDS):
            pl.when(jnp.abs(bed - b) == distance)(lambda b=b: centre(b).start())

    centres(1)
    widen(0)

    @by_group
    def _(q):
        for s in range(2):
            direct(q, *mirror, s).start()
        for s in range(2):
            direct(q, *near[1], s).start()

    centres(2)
    widen(1)
    centres(3)
    widen(2)
    widen(3)
    order = [other(bed, k) for k in (2, 3, 1)]

    @by_group
    def _(q):
        for s in range(2):
            take(q, *mirror, s)
            for b, r in near:
                relay(q, b, r, s).start()
            across(q, *mirror, s).start()

    for b in [order[1], order[0], order[2], bed]:
        pl.when(index(b, 1, core) != me)(lambda b=b: level(b, 3, 4, 1).start())
    for b in [order[1], order[0], order[2], bed]:
        pl.when(index(b, 0, core) != me)(lambda b=b: level(b, 0, 1, 0).start())
    for b in [order[1], order[0], order[2], bed]:
        pl.when((index(b, 0, 0) != me) & (b > 0))(lambda b=b: outer(b, -1, 0, 0).start())
    for b in [order[1], order[0], order[2], bed]:
        pl.when((index(b, 1, 1) != me) & (b < BEDS - 1))(lambda b=b: outer(b, 4, 5, 1).start())

    pass_on(near, range(2))
    for b in order[::-1]:
        arrived(cells.at[pl.ds(2, 2), :, slot(b, row, core)], centre_recv.at[b])
        turn(b).start()
    own_cells.wait()

    def quarter(r, c):
        return pl.ds(pl.multiple_of((c * 2 + r) * BEDS * cin, BEDS * cin), BEDS * cin)

    def mate(k):
        if k < 2:
            at = cells.at[pl.ds(2, 2), :, quarter(row if k == 0 else 1 - row, core)]
        else:
            at = cells.at[pl.ds(1 + 3 * row, 1), :, side(core)]
        return remote(at, at, csend.at[k], crecv.at[k], {"gx": partner})

    def mated(k):
        if k < 2:
            at = cells.at[pl.ds(2, 2), :, quarter(row if k == 0 else 1 - row, 1 - core)]
        else:
            at = cells.at[pl.ds(1 + 3 * row, 1), :, side(1 - core)]
        arrived(at, crecv.at[k])

    mate(0).start()
    pass_on(distant, range(2))
    own_weight.wait()
    by_group(lambda q: beside(q).start())
    arrived(cells.at[pl.ds(2, 2), :, quarter(1 - row, core)], turn_recv)
    mate(1).start()
    arrived(cells.at[pl.ds(1, 1), :, pl.ds(0, 7 * cin)], level_recv)
    mate(2).start()

    @by_group
    def _(q):
        arrived(weights.at[pl.ds(*cuts[1 - q]), pl.ds(0, 7 * cin)], xrecv)
        beside(1 - q).start()

    own_bias.wait()
    cout = weights.shape[2]
    local = 1 + row * 2 + core

    def turn_over(c):
        for tap in range(taps):
            kx, ky, kz = tap // 9, tap // 3 % 3, tap % 3
            turned[c, pl.ds(kz * cout, cout), pl.ds((kx * 3 + ky) * half, half)] = jnp.transpose(
                weights[tap, side(c)]
            )

    def product(c, low, high):
        zero = jnp.zeros((half, wide_z), cells.dtype)
        sides = []
        for kx in range(3):
            for ky in range(3):
                found = [
                    cells[local - 1 + kx, y + ky - 1, side(c)] if 0 <= y + ky - 1 < wide_y else zero
                    for y in range(low, high)
                ]
                sides.append(jnp.concatenate(found, axis=1))
        return jnp.dot(
            turned[c], jnp.concatenate(sides, axis=0), preferred_element_type=jnp.float32
        )

    @pl.when(starts & (bed > 0))
    def _():
        own_first().wait()

    @pl.when(ends & (bed < BEDS - 1))
    def _():
        own_last().wait()

    @pl.when((starts & (bed > 0)) | (ends & (bed < BEDS - 1)))
    def _():
        arrived(cells.at[pl.ds(0, 1), :, pl.ds(0, 15 * cin)], outer_recv)

    turn_over(core)
    for low, high in ((0, 2), (2, 4), (4, 6)):
        total[:, pl.ds(low * wide_z, (high - low) * wide_z)] = product(core, low, high)

    for q in range(2):
        arrived(weights.at[pl.ds(*cuts[q]), side(1 - core)], mrecv.at[q])
    turn_over(1 - core)
    for k in range(3):
        mated(k)

    def edge(k):
        low, high = SPANS[k]
        at = pl.ds(low, high - low)
        return remote(
            hidden.at[0, at], hidden.at[1, at], esend.at[k], erecv.at[k], {"gx": me - 1}
        )

    bias_cells = jnp.transpose(jnp.broadcast_to(bias_row[...], (wide_z, cout)))
    for k, (low, high) in enumerate(SPANS):
        final = total[:, pl.ds(low * wide_z, (high - low) * wide_z)] + product(1 - core, low, high)
        for y in range(low, high):
            part = final[:, (y - low) * wide_z : (y - low + 1) * wide_z]
            hidden[0, y] = jnp.maximum(
                part[cout : 2 * cout]
                + shift_up(part[:cout])
                + shift_down(part[2 * cout :])
                + bias_cells,
                0.0,
            ).astype(jnp.bfloat16)

        @pl.when(me > 0)
        def _(k=k):
            edge(k).start()

    own_fan.wait()
    spread = spreading(wide_z)

    def field(i):
        return lambda y: hidden[i, y]

    def write(pu, low, high):
        fields = ((1, field(0)),) if pu == 0 else ((2, field(0)), (0, field(1)))
        for v, value in upsampled(fields, fan, spread, low, high, wide_y, wide_z):
            out[pu, v] = value

    write(0, 0, wide_y)

    def sent(at, sem):
        pltpu.make_async_copy(at, at, sem).wait()

    by_group(lambda q: sent(weights.at[pl.ds(*cuts[q]), pl.ds(0, 14 * cin)], wsend))
    for q in range(2):
        beside(q).wait_send()
    sent(cells.at[pl.ds(2, 2), :, pl.ds(0, 7 * cin)], csem_send)
    sent(cells.at[pl.ds(1, 1), :, pl.ds(0, 7 * cin)], level_send)
    fewer = (starts & (bed > 0)) | (ends & (bed < BEDS - 1))

    @pl.when(fewer)
    def _():
        sent(cells.at[pl.ds(1, 1), :, pl.ds(0, 5 * cin)], outer_send)

    @pl.when(jnp.logical_not(fewer))
    def _():
        sent(cells.at[pl.ds(1, 1), :, pl.ds(0, 6 * cin)], outer_send)

    for k in range(3):
        mate(k).wait_send()

    for k, (low, high) in enumerate(SPANS):
        @pl.when(me < count - 1)
        def _(k=k, low=low, high=high):
            arrived(hidden.at[1, pl.ds(low, high - low)], erecv.at[k])

        write(1, *LAST[k])

    @pl.when(me > 0)
    def _():
        for k in range(parts):
            edge(k).wait_send()


def local_conv(planes, weight, bias, hidden_out):
    wide_y, wide_z = planes.shape[1], planes.shape[3]
    cells = [lambda y, kx=kx: planes[kx, y] for kx in range(3)]
    hidden_out[...] = conv_hidden(cells, wide_y, wide_z, lambda t: weight[t], bias[...])


def spreading(wide_z):
    row = lax.broadcasted_iota(jnp.int32, (2 * wide_z, 2 * wide_z), 0)
    col = lax.broadcasted_iota(jnp.int32, (2 * wide_z, 2 * wide_z), 1)
    return jnp.where(
        col == jnp.where(row < wide_z, 2 * row, 2 * (row - wide_z) + 1), 1.0, 0.0
    ).astype(jnp.bfloat16)


def upsampled(fields, tconv, spread, low, high, wide_y, wide_z):
    cup, cout = tconv.shape[1], tconv.shape[2]
    zero = jnp.zeros((cout, wide_z), jnp.bfloat16)
    found = []
    for pv in range(2):
        left, right = [], []
        for kx, field in fields:
            for ky, shift in (((1, 0),), ((2, 0), (0, 1)))[pv]:
                tap = kx * 9 + ky * 3
                left.append(tconv[tap : tap + 3].reshape(3 * cup, cout))
                right.append(
                    jnp.concatenate(
                        [
                            field(y + shift) if y + shift < wide_y else zero
                            for y in range(low, high)
                        ],
                        axis=1,
                    )
                )
        product = jnp.dot(
            jnp.concatenate(left, axis=1), jnp.concatenate(right, axis=0),
            preferred_element_type=jnp.float32,
        )
        pairs = []
        for i in range(high - low):
            part = product[:, i * wide_z : (i + 1) * wide_z]
            even = part[cup : 2 * cup]
            odd = part[2 * cup :] + shift_down(part[:cup])
            pairs.append(jnp.concatenate([even, odd], axis=1).astype(jnp.bfloat16))
        mixed = jnp.dot(
            jnp.concatenate(pairs, axis=0), spread, preferred_element_type=jnp.float32
        ).astype(jnp.bfloat16)
        for i in range(high - low):
            found.append((2 * (low + i) + pv, mixed[i * cup : (i + 1) * cup]))
    return found


def transposed(hidden, tconv, out):
    wide_y, wide_z = out.shape[1] // 2, out.shape[3] // 2
    spread = spreading(wide_z)

    def field(i):
        return lambda y: hidden[i, y]

    for pu in range(2):
        fields = ((1, field(0)),) if pu == 0 else ((2, field(0)), (0, field(1)))
        for v, value in upsampled(fields, tconv, spread, 0, wide_y, wide_y, wide_z):
            out[pu, v] = value


def native_hidden(volume, conv_weight, bias):
    count = lax.axis_size("gx")
    forward = [(i, i + 1) for i in range(count - 1)]
    backward = [(i + 1, i) for i in range(count - 1)]
    local = lax.all_to_all(volume, "gx", split_axis=0, concat_axis=1, tiled=True)
    weight = lax.all_gather(conv_weight, "gx", axis=0, tiled=True)
    rows = local.shape[0]
    low = lax.ppermute(local[rows - 1 :], "gx", forward)
    high = lax.ppermute(local[:1], "gx", backward)
    planes = jnp.transpose(jnp.concatenate([low, local, high], axis=0), (0, 2, 1, 3))
    weight = jnp.transpose(weight, (1, 0, 2))
    cout = weight.shape[2]
    shape = jax.ShapeDtypeStruct((cout, planes.shape[1] * planes.shape[3]), jnp.bfloat16)
    conv = pl.pallas_call(
        local_conv, out_shape=shape, in_specs=[VMEM] * 3, out_specs=VMEM,
        compiler_params=pltpu.CompilerParams(vmem_limit_bytes=40 << 20),
    )
    hidden = [conv(planes[r : r + 3], weight, bias) for r in range(rows)]
    hidden.append(lax.ppermute(hidden[0], "gx", backward))
    wide_y, wide_z = volume.shape[2], volume.shape[3]
    hidden = [
        jnp.transpose(plane.reshape(cout, wide_y, wide_z), (1, 0, 2)) for plane in hidden
    ]
    return [jnp.stack(hidden[r : r + 2]) for r in range(rows)]


def remote_decoded(volume, conv_weight, bias, tconv_weight):
    count = lax.axis_size("gx")
    cells = jnp.transpose(volume, (0, 2, 1, 3))
    weight = jnp.transpose(conv_weight, (1, 0, 2))
    taps, cin, cout = weight.shape
    wide_y, wide_z = cells.shape[1], cells.shape[3]
    wide = count * cin
    chips = count // 2
    parts = len(SPANS)
    dma = pltpu.SemaphoreType.DMA
    cup = tconv_weight.shape[1]
    shape = (2, 2 * wide_y, cup, 2 * wide_z)
    return pl.pallas_call(
        exchange_conv,
        out_shape=pltpu.VMEM(shape, jnp.bfloat16),
        in_specs=[HBM, HBM, HBM, HBM],
        out_specs=VMEM,
        scratch_shapes=[
            pltpu.VMEM((6, wide_y, wide, wide_z), jnp.bfloat16),
            pltpu.VMEM((taps, wide, cout), jnp.bfloat16),
            pltpu.VMEM((2, 3 * cout, 9 * wide // 2), jnp.bfloat16),
            pltpu.VMEM((3 * cout, wide_y * wide_z), jnp.float32),
            pltpu.VMEM((2, wide_y, cout, wide_z), jnp.bfloat16),
            pltpu.VMEM((1, cout), jnp.float32),
            pltpu.VMEM(tconv_weight.shape, jnp.bfloat16),
            dma((5,)),
            dma(()), dma((BEDS,)), dma(()), dma(()), dma(()), dma(()), dma(()),
            dma((3,)), dma((3,)),
            dma(()), dma((2, chips)), dma(()), dma((2,)), dma((2,)),
            dma((parts,)), dma((parts,)),
            pltpu.SemaphoreType.REGULAR((4,)),
        ],
        compiler_params=pltpu.CompilerParams(
            collective_id=0, has_side_effects=True, vmem_limit_bytes=44 << 20
        ),
    )(*(
        pltpu.with_memory_space_constraint(given, pltpu.HBM)
        for given in (cells, weight, bias.reshape(1, cout), tconv_weight)
    ))


def per_device(volume, conv_weight, conv_bias, tconv_weight):
    count = lax.axis_size("gx")
    rows = volume.shape[0] // count
    bias = conv_bias[:, None]
    suited = (
        rows == 1 and count == 16 and lax.axis_size("groups") == 2
        and volume.shape[1] % 16 == 0 and volume.shape[2] == SPANS[-1][1]
    )
    if suited:
        out = remote_decoded(volume, conv_weight, bias, tconv_weight)
        return jnp.transpose(out, (0, 2, 1, 3))
    cup = tconv_weight.shape[1]
    shape = jax.ShapeDtypeStruct(
        (2, 2 * volume.shape[2], cup, 2 * volume.shape[3]), jnp.bfloat16
    )
    tconv = pl.pallas_call(
        transposed, out_shape=shape, in_specs=[VMEM] * 2, out_specs=VMEM,
        compiler_params=pltpu.CompilerParams(vmem_limit_bytes=40 << 20),
    )
    hidden = native_hidden(volume, conv_weight, bias)
    out = jnp.concatenate([tconv(planes, tconv_weight) for planes in hidden], axis=0)
    return jnp.transpose(out, (0, 2, 1, 3))


def solution(mesh):
    return jax.shard_map(
        per_device,
        mesh=mesh,
        in_specs=(P("groups", "gx", None, None), P("gx", None, None), P(), P()),
        out_specs=P(("groups", "gx"), None, None, None),
        check_vma=False,
    )
```
